32 devices in a mesh: view: 4 (over y, x), point: 8 (over z, core).
Axes of the slice: x: 2, y: 2, z: 4, core: 2. Of those that a mesh axis runs over, the one named last changes fastest.
Arguments:
- features: bfloat16 [128, 32, 128, 256], P(('view', 'point')), may hold values from -6 to 6
- tiles: int32 [128, 2], P(('view', 'point')), may hold values from 0 to 7, as said below
- masks: int32 [128, 32, 128], P(('view', 'point')), may hold values from 0 to 1
- w_self: bfloat16 [3, 256, 256], replicated, may hold values from -0.375 to 0.375
- w_col: bfloat16 [3, 256, 256], replicated, may hold values from -0.09375 to 0.09375
- w_row: bfloat16 [3, 256, 256], replicated, may hold values from -0.03125 to 0.03125
- bias: float32 [3, 256], replicated, may hold values from -3 to 3
Outputs:
- result: bfloat16 [128, 32, 128, 256], P(('view', 'point'))
The draws below stay inside these ranges and needn't reach their ends.
Inputs may be any that keep to these rules, and one draw needn't show every extreme that they name: `tiles`: column 0 is a view tile of the slot's own view block, below 4. Column 1 below 4 is a point tile of the device's own point block; otherwise, minus 4, a point tile of the block of the next device along point, the last device's next being the first. No two slots name the same tile.
All inputs are finite; a program needn't handle non-finite values.
Results may differ from the reference program's by a relative error of at most 0.0051.
Values sent between devices are 32-bit elements; how exact they have to be, the bound alone decides.
A program may use at most 128 MiB of HBM per device.

```python
import jax
import jax.numpy as jnp
from jax import lax

D = 256
TV = 32
TP = 128
VT_DEV = 4
PT_DEV = 4
SLOTS = 4
LAYERS = 3
ALL_SLOTS = 128
N_VIEW = 4
N_POINT = 8


def tile_layout(key):
    base_key = jax.random.fold_in(key, 7)
    help_key, order_key = jax.random.split(base_key)
    cell_total = VT_DEV * PT_DEV
    helped = jax.random.randint(help_key, (N_VIEW, N_POINT), 0, SLOTS + 1).astype(jnp.int32)
    order_keys = jax.random.split(order_key, N_VIEW * N_POINT)
    cell_order = jax.vmap(lambda subkey: jax.random.permutation(subkey, cell_total))(order_keys)
    cell_order = cell_order.reshape(N_VIEW, N_POINT, cell_total).astype(jnp.int32)
    helped_after = jnp.roll(helped, -1, axis=1)
    owned = SLOTS - helped_after
    slot_index = jnp.arange(SLOTS, dtype=jnp.int32)[None, None, :]
    is_owned = slot_index < owned[..., None]
    own_pick = jnp.minimum(helped[..., None] + slot_index, cell_total - 1)
    after_pick = jnp.maximum(slot_index - owned[..., None], 0)
    order_after = jnp.roll(cell_order, -1, axis=1)
    own_cell = jnp.take_along_axis(cell_order, own_pick, axis=2)
    after_cell = jnp.take_along_axis(order_after, after_pick, axis=2)
    chosen = jnp.where(is_owned, own_cell, after_cell)
    offset = jnp.where(is_owned, 0, PT_DEV)
    view_column = chosen // PT_DEV
    point_column = chosen % PT_DEV + offset
    stacked = jnp.stack([view_column, point_column], axis=-1)
    return stacked.reshape(N_VIEW * N_POINT * SLOTS, 2).astype(jnp.int32)


def draw_tiles(key, part):
    return tile_layout(key)


def draw_masks(key, part):
    slot_ids = jnp.arange(ALL_SLOTS, dtype=jnp.int32)
    device_index = slot_ids // SLOTS
    view_pos = device_index // N_POINT
    point_pos = device_index % N_POINT
    threshold = 150 + 350 * point_pos // max(N_POINT - 1, 1) + 350 * view_pos // max(N_VIEW - 1, 1)
    drawn = jax.random.randint(jax.random.fold_in(key, 3), (ALL_SLOTS, TV, TP), 0, 1000)
    return (drawn < threshold[:, None, None]).astype(jnp.int32)


def block_scale(stream_key, shape, cuts, least, top_value):
    def one(axis_at, shards_of):
        steps = jax.random.uniform(jax.random.fold_in(jax.random.fold_in(stream_key, 6), axis_at), (shards_of,), jnp.float32, least / len(cuts), top_value / len(cuts))
        return jnp.repeat(jnp.exp(steps), shape[axis_at] // shards_of).reshape((-1,) + (1,) * (len(shape) - axis_at - 1))

    loudness = one(*cuts[0])
    for cut in cuts[1:]:
        loudness = loudness * one(*cut)
    return loudness


def scatter_about(stream_key, shape, width, reach, pieces=(), held_as=jnp.bfloat16):
    entries = jax.random.normal(stream_key, shape, jnp.float32) * width
    if len(pieces) > 0:
        entries = block_scale(stream_key, shape, pieces, -0.22, 0.18) * entries
    return jnp.clip(entries, min=-reach, max=reach).astype(held_as)


def setup_inputs(seed: int = 0) -> dict:
    seeds = jax.random.split(jax.random.key(seed), 8)
    return {
        "features": scatter_about(seeds[0], (ALL_SLOTS, TV, TP, D), 1.0, 6.0, ((0, 32),)),
        "tiles": draw_tiles(jax.random.fold_in(seeds[7], 71), 0),
        "masks": draw_masks(jax.random.fold_in(seeds[7], 71), 0),
        "w_self": scatter_about(seeds[3], (LAYERS, D, D), D ** -0.5, 0.375),
        "w_col": scatter_about(seeds[4], (LAYERS, D, D), (D * 16) ** -0.5, 0.09375),
        "w_row": scatter_about(seeds[5], (LAYERS, D, D), (D * 128) ** -0.5, 0.03125),
        "bias": scatter_about(seeds[6], (LAYERS, D), 0.5, 3.0, (), jnp.float32),
    }


def reference(features, tiles, masks, w_self, w_col, w_row, bias):
    device_index = jnp.arange(ALL_SLOTS, dtype=jnp.int32) // SLOTS
    view_pos = device_index // N_POINT
    point_pos = device_index % N_POINT
    view_tile = (view_pos * VT_DEV + tiles[:, 0]).astype(jnp.int32)
    point_tile = ((point_pos + tiles[:, 1] // PT_DEV) % N_POINT * PT_DEV + tiles[:, 1] % PT_DEV).astype(jnp.int32)
    view_tiles_all = VT_DEV * N_VIEW
    point_tiles_all = PT_DEV * N_POINT
    mask_f = masks.astype(jnp.float32)
    row_count = jax.ops.segment_sum(lax.optimization_barrier(jnp.sum(mask_f, axis=2)), view_tile, view_tiles_all)
    col_count = jax.ops.segment_sum(lax.optimization_barrier(jnp.sum(mask_f, axis=1)), point_tile, point_tiles_all)
    row_scale = 1.0 / jnp.sqrt(jnp.maximum(row_count, 1.0))
    col_scale = 1.0 / jnp.sqrt(jnp.maximum(col_count, 1.0))
    devices_all = ALL_SLOTS // SLOTS
    mask_blocks = masks.reshape(devices_all, SLOTS, TV, TP)
    view_blocks = view_tile.reshape(devices_all, SLOTS)
    point_blocks = point_tile.reshape(devices_all, SLOTS)
    current = features
    for layer_step in range(LAYERS):
        feat_blocks = current.reshape(devices_all, SLOTS, TV, TP, D)

        def slot_sums(block_args):
            block_feat, block_mask = block_args
            feat32 = block_feat.astype(jnp.float32)
            mask32 = block_mask.astype(jnp.float32)
            row_part = jnp.einsum('src,srcd->srd', mask32, feat32)
            col_part = jnp.einsum('src,srcd->scd', mask32, feat32)
            return (row_part, col_part)
        row_part, col_part = lax.map(slot_sums, (feat_blocks, mask_blocks))
        row_sum = jax.ops.segment_sum(row_part.reshape(ALL_SLOTS, TV, D), view_tile, view_tiles_all)
        col_sum = jax.ops.segment_sum(col_part.reshape(ALL_SLOTS, TP, D), point_tile, point_tiles_all)
        row_term = (row_sum * row_scale[..., None]).astype(jnp.bfloat16)
        col_term = (col_sum * col_scale[..., None]).astype(jnp.bfloat16)
        row_proj = jnp.dot(row_term.reshape(-1, D), w_row[layer_step], preferred_element_type=jnp.float32).reshape(view_tiles_all, TV, D)
        col_proj = jnp.dot(col_term.reshape(-1, D), w_col[layer_step], preferred_element_type=jnp.float32).reshape(point_tiles_all, TP, D)
        weight_self = w_self[layer_step]
        bias_row = bias[layer_step]

        def layer_block(block_args):
            block_feat, block_mask, block_view, block_point = block_args
            self_proj = jnp.dot(block_feat.reshape(-1, D), weight_self, preferred_element_type=jnp.float32).reshape(SLOTS, TV, TP, D)
            mixed_sum = self_proj + col_proj[block_point][:, None, :, :] + row_proj[block_view][:, :, None, :] + bias_row
            return (jnp.maximum(mixed_sum, 0.0) * block_mask.astype(jnp.float32)[..., None]).astype(jnp.bfloat16)
        current = lax.map(layer_block, (feat_blocks, mask_blocks, view_blocks, point_blocks)).reshape(ALL_SLOTS, TV, TP, D)
    return current
```

```python
import functools

import jax
import jax.numpy as jnp
from jax import lax
from jax.experimental import pallas as pl
from jax.experimental.pallas import tpu as pltpu
from jax.sharding import PartitionSpec as P

VT_DEV = 4
PT_DEV = 4
MESH = pl.DeviceIdType.MESH
F32 = jnp.float32
BF16 = jnp.bfloat16


def wide(x, width):
    reps = width // x.shape[-1]
    return x if reps == 1 else jnp.concatenate([x] * reps, axis=-1)


def stage_order(nk):
    stages = []
    for k in range(nk):
        ready = max(-2.0 + 5.7 * (k + 1) / nk, 0.0)
        stages.append((ready, 0, "sum", k))
        stages.append((max(ready, 0.2) + 3.5, 1, "project", k))
        stages.append((0.1 + 2.2 * k / nk, 2, "self", k))
    stages.append((4.6, 3, "row", 0))
    return [(name, k) for _, _, name, k in sorted(stages)]


def layers_kernel(
    nv, np_, nk,
    tiles_ref, feat_ref, mask_hbm, wself_hbm, wcol_hbm, wrow_hbm, bias_ref,
    cur,
    mask_ref, wself_ref, wcol_ref, wrow_ref, self_p, pick, gather_mat, scatter_mat,
    col_send, rs_buf, total_buf, side_buf, ag_send, ag_buf,
    row_acc, row_send, row_rs, row_ag_send, row_ag, row_p,
    cm_send, cm_buf, ri_send, ri_buf, col_scale, row_scale,
    feat_sem, in_sem, rs_s, rs_r, f_s, f_r, b_s, b_r, ag_s, ag_r,
    rr_s, rr_r, ra_s, ra_r, cm_s, cm_r, ri_s, ri_r,
):
    a = lax.axis_index("view")
    b = lax.axis_index("point")
    slots, rows, cols, width = cur.shape
    layers = wself_ref.shape[0]
    chunk = cols // nk
    part = chunk // nv
    share = row_send.shape[1]
    tiles_near = 2 * PT_DEV

    def view_at(o):
        return lax.rem(a + o, nv)

    def point_at(o):
        return lax.rem(b + o + np_, np_)

    def remote(src, dst, ssem, rsem, va, pb):
        return pltpu.make_async_remote_copy(
            src_ref=src, dst_ref=dst, send_sem=ssem, recv_sem=rsem,
            device_id=(va, pb), device_id_type=MESH,
        )

    def rs_copy(k, o):
        return remote(col_send.at[k, view_at(o)], rs_buf.at[k, o - 1],
                      rs_s.at[k, o - 1], rs_r.at[k, o - 1], view_at(o), b)

    def ag_copy(k, o):
        return remote(ag_send.at[k, o - 1], ag_buf.at[k, o],
                      ag_s.at[k, o - 1], ag_r.at[k, o - 1], view_at(o), b)

    def f_copy(turn, k):
        return remote(total_buf.at[k, pl.ds(PT_DEV, PT_DEV)], side_buf.at[turn, k, pl.ds(0, PT_DEV)],
                      f_s.at[turn, k], f_r.at[turn, k], a, point_at(1))

    def b_copy(turn, k):
        return remote(total_buf.at[k, pl.ds(0, PT_DEV)], side_buf.at[turn, k, pl.ds(PT_DEV, PT_DEV)],
                      b_s.at[turn, k], b_r.at[turn, k], a, point_at(-1))

    def rr_copy(o):
        return remote(row_send.at[point_at(o)], row_rs.at[o - 1],
                      rr_s.at[o - 1], rr_r.at[o - 1], a, point_at(o))

    def ra_copy(o):
        return remote(row_ag_send, row_ag.at[o - 1], ra_s.at[o - 1], ra_r.at[o - 1], a, point_at(o))

    near = [(o, d) for d in (0, 1, -1) for o in range(nv) if (o, d) != (0, 0)]

    def cm_copy(n):
        o, d = near[n]
        return remote(cm_send, cm_buf.at[n], cm_s.at[n], cm_r.at[n], view_at(o), point_at(d))

    def ri_copy(o):
        return remote(ri_send.at[point_at(o)], ri_buf.at[o - 1],
                      ri_s.at[o - 1], ri_r.at[o - 1], a, point_at(o))

    def feat_copy(k):
        span = pl.ds(k * chunk, chunk)
        return pltpu.make_async_copy(
            feat_ref.at[:, :, span, :], cur.at[:, :, span, :], feat_sem.at[k])

    def in_copy(n):
        src = (mask_hbm, wself_hbm, wcol_hbm, wrow_hbm)[n]
        dst = (mask_ref, wself_ref, wcol_ref, wrow_ref)[n]
        return pltpu.make_async_copy(src, dst, in_sem.at[n])

    in_copy(0).start()
    for k in range(nk):
        feat_copy(k).start()
    for n in range(1, 4):
        in_copy(n).start()

    barrier = pltpu.get_barrier_semaphore()
    friends = [(0, o) for o in range(2, np_ - 1)] + near
    for o, d in friends:
        pl.semaphore_signal(barrier, inc=1, device_id=(view_at(o), point_at(d)) if (o, d) in near
                            else (a, point_at(d)), device_id_type=MESH)
    in_copy(0).wait()

    group = pick.shape[4] // chunk
    lanes = cols

    for s in range(slots):
        cm_send[s:s + 1, :] = jnp.sum(mask_ref[s].astype(F32), axis=0, keepdims=True)
        cm_send[slots + s:slots + s + 1, :] = jnp.full(
            (1, lanes), tiles_ref[1, s], jnp.int32).astype(F32)
    for v in range(VT_DEV):
        total = jnp.zeros((rows, lanes), F32)
        for s in range(slots):
            rcount = jnp.broadcast_to(
                jnp.sum(mask_ref[s].astype(F32), axis=1, keepdims=True), (rows, lanes))
            hit = jnp.full((rows, lanes), tiles_ref[0, s], jnp.int32) == v
            total = total + jnp.where(hit, rcount, 0.0)
        for i in range(max(rows // share, 1)):
            at = v * rows + i * share
            ri_send[at // share] = total[i * share:(i + 1) * share]

    def build_pick(s, carry):
        shape = (group, group * chunk)
        lane = lax.broadcasted_iota(jnp.int32, shape, 1)
        of_view = lane // chunk == lax.broadcasted_iota(jnp.int32, shape, 0)
        shape = (chunk, group * chunk)
        lane = lax.broadcasted_iota(jnp.int32, shape, 1)
        of_point = lane % chunk == lax.broadcasted_iota(jnp.int32, shape, 0)
        for g in range(rows // group):
            m = mask_ref[s, g * group:(g + 1) * group, :].astype(F32)
            for k in range(nk):
                tiled = jnp.concatenate([m[:, k * chunk:(k + 1) * chunk]] * group, axis=1)
                by_view = jnp.where(of_view, tiled, 0.0)
                flat = jnp.sum(by_view, axis=0, keepdims=True)
                by_point = jnp.where(of_point, jnp.broadcast_to(flat, shape), 0.0)
                both = jnp.concatenate([by_point, by_view, jnp.zeros_like(by_view)], axis=0)
                pick[s, k, g] = both.astype(BF16)
        return carry

    lax.fori_loop(0, slots, build_pick, 0)

    def sum_rows(k, s, value_of):
        col = jnp.zeros((chunk, width), F32)
        for g in range(rows // group):
            both = jnp.dot(pick[s, k, g], value_of(g), preferred_element_type=F32)
            col = col + both[:chunk]
            new = both[chunk:chunk + group]
            at = pl.ds(g * group, group)
            if k == 0:
                row_acc[s, at, :] = new
            else:
                row_acc[s, at, :] = row_acc[s, at, :] + new
        for j in range(nv):
            col_send[k, j, s] = col[j * part:(j + 1) * part]

    def entries(k, s, g):
        span = pl.ds(k * chunk, chunk)
        return cur[s, g * group:(g + 1) * group, span, :].reshape(group * chunk, width)

    def over_slots(slot):
        lax.fori_loop(0, slots, slot, 0, unroll=4 if slots % 4 == 0 else 1)

    def first_sums(k):
        def slot(s, carry):
            sum_rows(k, s, lambda g: entries(k, s, g))
            return carry
        over_slots(slot)

    def self_project(layer, k):
        span = pl.ds(k * chunk, chunk)

        def slot(s, carry):
            for g in range(rows // group):
                z = jnp.dot(entries(k, s, g), wself_ref[layer], preferred_element_type=F32)
                self_p[s, g * group:(g + 1) * group, span, :] = z.reshape(group, chunk, width)
            return carry
        over_slots(slot)

    def mixed(k, s, g, colp, rowp):
        z = self_p[s, g * group:(g + 1) * group, pl.ds(k * chunk, chunk), :]
        return jnp.maximum(z + colp[None] + rowp[g * group:(g + 1) * group][:, None, :], 0.0)

    def terms(k, s):
        colp = jnp.concatenate(
            [ag_buf[k, lax.rem(a - j + nv, nv), s] for j in range(nv)], axis=0)
        return colp, row_p[tiles_ref[0, s]]

    def layer_chunk(k):
        def slot(s, carry):
            colp, rowp = terms(k, s)

            def value_of(g):
                y = mixed(k, s, g, colp, rowp).astype(BF16)
                cur[s, g * group:(g + 1) * group, pl.ds(k * chunk, chunk), :] = y
                return y.reshape(group * chunk, width)
            sum_rows(k, s, value_of)
            return carry
        over_slots(slot)

    def last_chunk(k):
        def slot(s, carry):
            colp, rowp = terms(k, s)
            mt = mask_ref[s].astype(F32).T[k * chunk:(k + 1) * chunk]
            for g in range(rows // group):
                y = mixed(k, s, g, colp, rowp)
                for i in range(group):
                    r = g * group + i
                    m = jnp.broadcast_to(mt[:, r:r + 1], (chunk, width))
                    cur[s, r, pl.ds(k * chunk, chunk), :] = (y[i] * m).astype(BF16)
            return carry
        lax.fori_loop(0, slots, slot, 0)

    def send_rows():
        for v in range(VT_DEV):
            total = jnp.zeros((rows, width), F32)
            for s in range(slots):
                hit = jnp.full((rows, width), tiles_ref[0, s], jnp.int32) == v
                total = total + jnp.where(hit, row_acc[s], 0.0)
            for i in range(max(rows // share, 1)):
                at = v * rows + i * share
                row_send[at // share] = total[i * share:(i + 1) * share]
        for o in range(1, np_):
            rr_copy(o).start()

    def send_cols(k):
        for o in range(1, nv):
            rs_copy(k, o).start()

    def halves(x):
        high = x.astype(BF16)
        return jnp.concatenate([high, (x - high.astype(F32)).astype(BF16)], axis=0)

    for k in range(nk):
        feat_copy(k).wait()
        first_sums(k)
        if k == 0:
            pl.semaphore_wait(barrier, len(friends))
            for n in range(len(near)):
                cm_copy(n).start()
        if k == nk - 1:
            send_rows()
        send_cols(k)
    for o in range(1, np_):
        ri_copy(o).start()
    for n in range(1, 4):
        in_copy(n).wait()

    for n in range(len(near)):
        cm_copy(n).wait()
    messages = {(0, 0): cm_send[...]}
    for n, at in enumerate(near):
        messages[at] = cm_buf[n]

    def tile_of(o, s):
        return messages[o, 0][slots + s:slots + s + 1, :]

    def lane_tiled(x, size):
        return x[:, :size] if size <= lanes else jnp.concatenate([x] * (size // lanes), axis=1)

    shape = scatter_mat.shape
    lane = lax.broadcasted_iota(jnp.int32, (1, shape[1]), 1) % (nv * slots * part)
    q_lane = jnp.zeros((1, shape[1]), F32)
    for o in range(nv):
        for s in range(slots):
            q_lane = jnp.where(lane // part == o * slots + s, lane_tiled(tile_of(o, s), shape[1]), q_lane)
    row = lax.broadcasted_iota(jnp.int32, shape, 0)
    lane = lax.broadcasted_iota(jnp.int32, shape, 1)
    hit = (jnp.broadcast_to(q_lane, shape) == (row // part).astype(F32)) & (row % part == lane % part)
    scatter_mat[...] = jnp.where(hit, 1.0, 0.0).astype(BF16)

    shape = (part, tiles_near * part)
    lane = lax.broadcasted_iota(jnp.int32, shape, 1)
    same = lane % part == lax.broadcasted_iota(jnp.int32, shape, 0)
    tile = (lane // part).astype(F32)
    found = []
    for o in range(nv):
        for s in range(slots):
            q = jnp.broadcast_to(lane_tiled(tile_of((nv - o) % nv, s), shape[1]), shape)
            found.append(jnp.where((q == tile) & same, 1.0, 0.0))
    gather_mat[...] = jnp.concatenate(found, axis=0).astype(BF16)

    shape = (tiles_near, lanes)
    tile = lax.broadcasted_iota(jnp.int32, shape, 0).astype(F32)
    count = jnp.zeros(shape, F32)
    for (o, d), block in messages.items():
        for s in range(slots):
            q = jnp.broadcast_to(block[slots + s:slots + s + 1, :], shape)
            hit = q - float(d * PT_DEV) == tile
            count = count + jnp.where(hit, jnp.broadcast_to(block[s:s + 1, :], shape), 0.0)
    scale = (1.0 / jnp.sqrt(jnp.maximum(count, 1.0))).T
    for t in range(tiles_near):
        col_scale[t] = jnp.broadcast_to(scale[:, t:t + 1], (cols, lanes))

    for o in range(1, np_):
        ri_copy(o).wait()
    total = ri_send[b]
    for o in range(1, np_):
        total = total + ri_buf[o - 1]
    row_scale[...] = wide(1.0 / jnp.sqrt(jnp.maximum(total, 1.0)), width)

    def stage_sum(turn, k):
        for o in range(1, nv):
            rs_copy(k, o).wait()
        blocks = [col_send[k, a] if o == 0 else rs_buf[k, o - 1] for o in range(nv)]
        blocks = jnp.concatenate([x.reshape(slots * part, width) for x in blocks], axis=0)
        total = jnp.dot(scatter_mat[...], halves(blocks), preferred_element_type=F32)
        total_buf[k] = total.reshape(tiles_near, part, width)
        f_copy(turn, k).start()
        b_copy(turn, k).start()

    def stage_project(layer, turn, k):
        f_copy(turn, k).wait()
        b_copy(turn, k).wait()
        at = pl.multiple_of(k * chunk + a * part, part)
        scale = wide(col_scale[:, pl.ds(at, part), :], width)
        term = (total_buf[k] + side_buf[turn, k]) * scale
        term = term.reshape(tiles_near * part, width).astype(BF16)
        term = jnp.dot(gather_mat[...], term, preferred_element_type=F32).astype(BF16)
        chosen = jnp.dot(term, wcol_ref[layer], preferred_element_type=F32)
        chosen = chosen.reshape(nv, slots, part, width)
        ag_buf[k, 0] = chosen[0]
        for o in range(1, nv):
            ag_send[k, o - 1] = chosen[o]
            ag_copy(k, o).start()

    def stage_row_project(layer):
        for o in range(1, np_):
            rr_copy(o).wait()
        total = row_send[b]
        for o in range(1, np_):
            total = total + row_rs[o - 1]
        term = (total * row_scale[...]).astype(BF16)
        row_ag_send[...] = (
            jnp.dot(term, wrow_ref[layer], preferred_element_type=F32)
            + bias_ref[pl.ds(layer, 1), :])
        for o in range(1, np_):
            ra_copy(o).start()

    def stage_row_collect():
        for o in range(1, np_):
            ra_copy(o).wait()

        for j in range(np_):
            o = lax.rem(b - j + np_, np_)
            got = row_ag[jnp.maximum(o - 1, 0)]
            block = jnp.where(jnp.full(got.shape, o, jnp.int32) == 0, row_ag_send[...], got)
            at = j * share
            row_p[at // rows, at % rows:at % rows + share, :] = block

    def exchange(layer, carry):
        turn = lax.rem(layer, 2)
        for name, k in stage_order(nk):
            if name == "sum":
                stage_sum(turn, k)
            elif name == "project":
                stage_project(layer, turn, k)
            elif name == "self":
                self_project(layer, k)
            else:
                stage_row_project(layer)
        stage_row_collect()
        for k in range(nk):
            for o in range(1, nv):
                ag_copy(k, o).wait()

            @pl.when(layer < layers - 1)
            def _():
                layer_chunk(k)
                if k == nk - 1:
                    send_rows()
                send_cols(k)

            @pl.when(layer == layers - 1)
            def _():
                last_chunk(k)
        return carry

    lax.fori_loop(0, layers, exchange, 0)


def hand_over_kernel(cur_ref, out_ref, sem):
    copies = [pltpu.make_async_copy(cur_ref.at[s], out_ref.at[s], sem.at[s])
              for s in range(cur_ref.shape[0])]
    for copy in copies:
        copy.start()
    for copy in copies:
        copy.wait()


def shards(nv, np_, features, tiles, masks, w_self, w_col, w_row, bias):
    slots, rows, cols, width = features.shape
    layers = w_self.shape[0]
    nk = max(cols // (8 * nv), 1)
    chunk = cols // nk
    part = chunk // nv
    share = VT_DEV * rows // np_
    group = 256 // chunk
    near = 3 * nv - 1
    tiles_near = 2 * PT_DEV
    vmem = pltpu.VMEM
    dma = pltpu.SemaphoreType.DMA
    whole = pl.BlockSpec(memory_space=pltpu.VMEM)
    away = pl.BlockSpec(memory_space=pltpu.HBM)
    scratch = [
        vmem(masks.shape, jnp.int32),
        vmem(w_self.shape, BF16),
        vmem(w_col.shape, BF16),
        vmem(w_row.shape, BF16),
        vmem((slots, rows, cols, width), F32),
        vmem((slots, nk, rows // group, chunk + 2 * group, group * chunk), BF16),
        vmem((nv * slots * part, tiles_near * part), BF16),
        vmem((tiles_near * part, 2 * nv * slots * part), BF16),
        vmem((nk, nv, slots, part, width), F32),
        vmem((nk, nv - 1, slots, part, width), F32),
        vmem((nk, tiles_near, part, width), F32),
        vmem((2, nk, tiles_near, part, width), F32),
        vmem((nk, nv - 1, slots, part, width), F32),
        vmem((nk, nv, slots, part, width), F32),
        vmem((slots, rows, width), F32),
        vmem((np_, share, width), F32),
        vmem((np_ - 1, share, width), F32),
        vmem((share, width), F32),
        vmem((np_ - 1, share, width), F32),
        vmem((VT_DEV, rows, width), F32),
        vmem((2 * slots, cols), F32),
        vmem((near, 2 * slots, cols), F32),
        vmem((np_, share, cols), F32),
        vmem((np_ - 1, share, cols), F32),
        vmem((tiles_near, cols, cols), F32),
        vmem((share, width), F32),
        dma((nk,)),
        dma((4,)),
        dma((nk, nv - 1)), dma((nk, nv - 1)),
        dma((2, nk)), dma((2, nk)), dma((2, nk)), dma((2, nk)),
        dma((nk, nv - 1)), dma((nk, nv - 1)),
        dma((np_ - 1,)), dma((np_ - 1,)), dma((np_ - 1,)), dma((np_ - 1,)),
        dma((near,)), dma((near,)),
        dma((np_ - 1,)), dma((np_ - 1,)),
    ]
    current = pl.pallas_call(
        functools.partial(layers_kernel, nv, np_, nk),
        out_shape=jax.ShapeDtypeStruct(features.shape, BF16),
        in_specs=[
            pl.BlockSpec(memory_space=pltpu.SMEM),
            away, away, away, away, away, whole,
        ],
        out_specs=whole,
        scratch_shapes=scratch,
        compiler_params=pltpu.CompilerParams(
            collective_id=0, has_side_effects=True, vmem_limit_bytes=44 * 1024 * 1024),
        name="layers",
    )(*[pltpu.with_memory_space_constraint(x, pltpu.HBM)
        for x in (tiles.T, features, masks, w_self, w_col, w_row, bias)])
    return pl.pallas_call(
        hand_over_kernel,
        out_shape=jax.ShapeDtypeStruct(features.shape, BF16),
        in_specs=[pl.BlockSpec(memory_space=pl.ANY)],
        out_specs=away,
        scratch_shapes=[dma((slots,))],
        compiler_params=pltpu.CompilerParams(vmem_limit_bytes=1024 * 1024),
        name="hand_over",
    )(current)


def solution(mesh):
    in_specs = (
        P(("view", "point"), None, None, None),
        P(("view", "point"), None),
        P(("view", "point"), None, None),
        P(), P(), P(), P(),
    )
    out_specs = P(("view", "point"), None, None, None)
    body = functools.partial(shards, mesh.shape["view"], mesh.shape["point"])
    return jax.shard_map(body, mesh=mesh, in_specs=in_specs, out_specs=out_specs, check_vma=False)
```

```python
import functools

import jax
import jax.numpy as jnp
from jax import lax
from jax.experimental import pallas as pl
from jax.experimental.pallas import tpu as pltpu
from jax.sharding import PartitionSpec as P

VT_DEV = 4
PT_DEV = 4
MESH = pl.DeviceIdType.MESH
F32 = jnp.float32
BF16 = jnp.bfloat16
BIG = 2.0 ** 100


def wide(x, width):
    reps = width // x.shape[-1]
    return x if reps == 1 else jnp.concatenate([x] * reps, axis=-1)


def stage_order(nk):
    stages = [(1.35, "tables", 0), (4.6, "row", 0)]
    for k in range(nk):
        ready = 1.4 + 3.1 * k / max(nk - 1, 1)
        stages.append((3.0 * k / nk, "self", k))
        stages.append((ready, "sum", k))
        stages.append((ready + 3.5, "project", k))
    for i, at in enumerate((4.7, 7.7, 8.5, 8.6)):
        stages.append((at, "bound", i))
    return [(name, k) for _, name, k in sorted(stages)]


def layers_kernel(
    nv, np_, nk,
    tiles_ref, feat_ref, mask_hbm, wself_hbm, wcol_hbm, wrow_hbm, bias_ref,
    cur,
    mask_ref, wself_ref, wcol_ref, wrow_ref, self_p, bound, pick, gather_mat, scatter_mat,
    col_send, rs_buf, total_buf, side_buf, ag_send, ag_buf,
    row_acc, row_send, row_rs, row_ag_send, row_ag, row_p,
    cm_send, cm_buf, ri_send, ri_buf, col_scale, row_scale,
    feat_sem, in_sem, rs_sem, side_sem, ag_sem, rr_sem, ra_sem, cm_sem, ri_sem,
):
    a = lax.axis_index("view")
    b = lax.axis_index("point")
    slots, rows, cols, width = cur.shape
    layers = wself_ref.shape[0]
    chunk = cols // nk
    part = chunk // nv
    share = row_send.shape[1]
    tiles_near = 2 * PT_DEV

    def view_at(o):
        return lax.rem(a + o, nv)

    def point_at(o):
        return lax.rem(b + o + np_, np_)

    def remote(src, dst, sems, va, pb):
        return pltpu.make_async_remote_copy(
            src_ref=src, dst_ref=dst, send_sem=sems.at[0], recv_sem=sems.at[1],
            device_id=(va, pb), device_id_type=MESH,
        )

    def wait_all(landed, sems):
        for end in range(2):
            pltpu.make_async_copy(landed, landed, sems.at[end]).wait()

    def rs_copy(k, o):
        return remote(col_send.at[k, view_at(o)], rs_buf.at[k, o - 1],
                      rs_sem.at[k], view_at(o), b)

    def ag_copy(k, o):
        return remote(ag_send.at[k, o - 1], ag_buf.at[k, o],
                      ag_sem.at[k], view_at(o), b)

    def f_copy(turn, k):
        return remote(total_buf.at[k, pl.ds(PT_DEV, PT_DEV)], side_buf.at[turn, k, pl.ds(0, PT_DEV)],
                      side_sem.at[turn, k], a, point_at(1))

    def b_copy(turn, k):
        return remote(total_buf.at[k, pl.ds(0, PT_DEV)], side_buf.at[turn, k, pl.ds(PT_DEV, PT_DEV)],
                      side_sem.at[turn, k], a, point_at(-1))

    def rr_copy(o):
        return remote(row_send.at[point_at(o)], row_rs.at[o - 1],
                      rr_sem, a, point_at(o))

    def ra_copy(o):
        return remote(row_ag_send, row_ag.at[o - 1], ra_sem, a, point_at(o))

    near = [(o, d) for d in (0, 1, -1) for o in range(nv) if (o, d) != (0, 0)]

    def cm_copy(n):
        o, d = near[n]
        return remote(cm_send, cm_buf.at[n], cm_sem, view_at(o), point_at(d))

    def ri_copy(o):
        return remote(ri_send.at[point_at(o)], ri_buf.at[o - 1],
                      ri_sem, a, point_at(o))

    def feat_copy(k):
        span = pl.ds(k * chunk, chunk)
        return pltpu.make_async_copy(
            feat_ref.at[:, :, span, :], cur.at[:, :, span, :], feat_sem.at[k])

    def in_copy(n):
        src = (mask_hbm, wself_hbm, wcol_hbm, wrow_hbm)[n]
        dst = (mask_ref, wself_ref, wcol_ref, wrow_ref)[n]
        return pltpu.make_async_copy(src, dst, in_sem.at[n])

    in_copy(0).start()
    for k in range(nk):
        feat_copy(k).start()
    for n in range(1, 4):
        in_copy(n).start()

    barrier = pltpu.get_barrier_semaphore()
    friends = [(0, o) for o in range(2, np_ - 1)] + near
    for o, d in friends:
        pl.semaphore_signal(barrier, inc=1, device_id=(view_at(o), point_at(d)) if (o, d) in near
                            else (a, point_at(d)), device_id_type=MESH)
    in_copy(0).wait()

    group = pick.shape[4] // chunk
    lanes = cols

    for s in range(slots):
        cm_send[s:s + 1, :] = jnp.sum(mask_ref[s].astype(F32), axis=0, keepdims=True)
        cm_send[slots + s:slots + s + 1, :] = jnp.full(
            (1, lanes), tiles_ref[1, s], jnp.int32).astype(F32)
    for v in range(VT_DEV):
        total = jnp.zeros((rows, lanes), F32)
        for s in range(slots):
            rcount = jnp.broadcast_to(
                jnp.sum(mask_ref[s].astype(F32), axis=1, keepdims=True), (rows, lanes))
            hit = jnp.full((rows, lanes), tiles_ref[0, s], jnp.int32) == v
            total = total + jnp.where(hit, rcount, 0.0)
        for i in range(max(rows // share, 1)):
            at = v * rows + i * share
            ri_send[at // share] = total[i * share:(i + 1) * share]

    def build_pick(s, carry):
        shape = (group, group * chunk)
        lane = lax.broadcasted_iota(jnp.int32, shape, 1)
        of_view = lane // chunk == lax.broadcasted_iota(jnp.int32, shape, 0)
        shape = (chunk, group * chunk)
        lane = lax.broadcasted_iota(jnp.int32, shape, 1)
        of_point = lane % chunk == lax.broadcasted_iota(jnp.int32, shape, 0)
        for g in range(rows // group):
            m = mask_ref[s, g * group:(g + 1) * group, :].astype(F32)
            for k in range(nk):
                tiled = jnp.concatenate([m[:, k * chunk:(k + 1) * chunk]] * group, axis=1)
                by_view = jnp.where(of_view, tiled, 0.0)
                flat = jnp.sum(by_view, axis=0, keepdims=True)
                by_point = jnp.where(of_point, jnp.broadcast_to(flat, shape), 0.0)
                both = jnp.concatenate([by_point, by_view, jnp.ones_like(by_view)], axis=0)
                pick[s, k, g] = both.astype(BF16)
        return carry

    lax.fori_loop(0, slots, build_pick, 0)

    def sum_rows(k, s, value_of):
        col = jnp.zeros((chunk, width), F32)
        for g in range(rows // group):
            both = jnp.dot(pick[s, k, g], value_of(g), preferred_element_type=F32)
            col = col + both[:chunk]
            new = both[chunk:chunk + group]
            at = pl.ds(g * group, group)
            if k == 0:
                row_acc[s, at, :] = new
            else:
                row_acc[s, at, :] = row_acc[s, at, :] + new
        for j in range(nv):
            col_send[k, j, s] = col[j * part:(j + 1) * part]

    def entries(k, s, g):
        span = pl.ds(k * chunk, chunk)
        return cur[s, g * group:(g + 1) * group, span, :].reshape(group * chunk, width)

    def over_slots(slot):
        lax.fori_loop(0, slots, slot, 0, unroll=4 if slots % 4 == 0 else 1)

    def first_sums(k):
        def slot(s, carry):
            sum_rows(k, s, lambda g: entries(k, s, g))
            return carry
        over_slots(slot)

    def build_bound(k, half):
        shape = (2 * group, bound.shape[3])
        row = lax.broadcasted_iota(jnp.int32, shape, 0)
        ends = jnp.where(row < group, 2.0 * BIG, jnp.where(row == group, -BIG, 0.0)).astype(BF16)

        def slot(s, carry):
            for g in range(rows // group):
                x = lax.dot_general(
                    pick[s, k, g, chunk:, :], ends, (((0,), (0,)), ((), ())),
                    preferred_element_type=F32)
                bound[s, g * group:(g + 1) * group, pl.ds(k * chunk, chunk), :] = (
                    x.reshape(group, chunk, shape[1]).astype(BF16))
            return carry
        lax.fori_loop(half * slots // 2, (half + 1) * slots // 2, slot, 0)

    def self_project(layer, k, masked):
        span = pl.ds(k * chunk, chunk)

        def slot(s, carry):
            for g in range(rows // group):
                z = jnp.dot(entries(k, s, g), wself_ref[layer], preferred_element_type=F32)
                z = z.reshape(group, chunk, width)
                if masked:
                    z = jnp.minimum(z, wide(
                        bound[s, g * group:(g + 1) * group, span, :].astype(F32), width))
                self_p[s, g * group:(g + 1) * group, span, :] = z
            return carry
        over_slots(slot)

    def mixed(k, s, g, colp, rowp):
        z = self_p[s, g * group:(g + 1) * group, pl.ds(k * chunk, chunk), :]
        z = z + colp[None] + rowp[g * group:(g + 1) * group][:, None, :]
        return jnp.maximum(z.astype(BF16), 0)

    def terms(k, s):
        colp = jnp.concatenate(
            [ag_buf[k, lax.rem(a - j + nv, nv), s] for j in range(nv)], axis=0)
        return colp, row_p[tiles_ref[0, s]]

    def layer_chunk(k):
        def slot(s, carry):
            colp, rowp = terms(k, s)

            def value_of(g):
                y = mixed(k, s, g, colp, rowp)
                cur[s, g * group:(g + 1) * group, pl.ds(k * chunk, chunk), :] = y
                return y.reshape(group * chunk, width)
            sum_rows(k, s, value_of)
            return carry
        over_slots(slot)

    def last_chunk(k):
        def slot(s, carry):
            colp, rowp = terms(k, s)
            for g in range(rows // group):
                y = mixed(k, s, g, colp, rowp)
                cur[s, g * group:(g + 1) * group, pl.ds(k * chunk, chunk), :] = y
            return carry
        over_slots(slot)

    def send_rows():
        for v in range(VT_DEV):
            total = jnp.zeros((rows, width), F32)
            for s in range(slots):
                hit = jnp.full((rows, width), tiles_ref[0, s], jnp.int32) == v
                total = total + jnp.where(hit, row_acc[s], 0.0)
            for i in range(max(rows // share, 1)):
                at = v * rows + i * share
                row_send[at // share] = total[i * share:(i + 1) * share]
        for o in range(1, np_):
            rr_copy(o).start()

    def send_cols(k):
        for o in range(1, nv):
            rs_copy(k, o).start()

    def halves(x):
        high = x.astype(BF16)
        return jnp.concatenate([high, (x - high.astype(F32)).astype(BF16)], axis=0)

    for k in range(nk):
        feat_copy(k).wait()
        first_sums(k)
        if k == 0:
            pl.semaphore_wait(barrier, len(friends))
            for n in range(len(near)):
                cm_copy(n).start()
            for o in range(1, np_):
                ri_copy(o).start()
        if k == nk - 1:
            send_rows()
        send_cols(k)
    for n in range(1, 4):
        in_copy(n).wait()

    def stage_tables():
        wait_all(cm_buf, cm_sem)
        messages = {(0, 0): cm_send[...]}
        for n, at in enumerate(near):
            messages[at] = cm_buf[n]

        def tile_of(o, s):
            return messages[o, 0][slots + s:slots + s + 1, :]

        def lane_tiled(x, size):
            return x[:, :size] if size <= lanes else jnp.concatenate([x] * (size // lanes), axis=1)

        shape = scatter_mat.shape
        lane = lax.broadcasted_iota(jnp.int32, (1, shape[1]), 1) % (nv * slots * part)
        q_lane = jnp.zeros((1, shape[1]), F32)
        for o in range(nv):
            for s in range(slots):
                q_lane = jnp.where(lane // part == o * slots + s, lane_tiled(tile_of(o, s), shape[1]), q_lane)
        row = lax.broadcasted_iota(jnp.int32, shape, 0)
        lane = lax.broadcasted_iota(jnp.int32, shape, 1)
        hit = (jnp.broadcast_to(q_lane, shape) == (row // part).astype(F32)) & (row % part == lane % part)
        scatter_mat[...] = jnp.where(hit, 1.0, 0.0).astype(BF16)

        shape = (part, tiles_near * part)
        lane = lax.broadcasted_iota(jnp.int32, shape, 1)
        same = lane % part == lax.broadcasted_iota(jnp.int32, shape, 0)
        tile = (lane // part).astype(F32)
        found = []
        for o in range(nv):
            for s in range(slots):
                q = jnp.broadcast_to(lane_tiled(tile_of((nv - o) % nv, s), shape[1]), shape)
                found.append(jnp.where((q == tile) & same, 1.0, 0.0))
        gather_mat[...] = jnp.concatenate(found, axis=0).astype(BF16)

        shape = (tiles_near, lanes)
        tile = lax.broadcasted_iota(jnp.int32, shape, 0).astype(F32)
        count = jnp.zeros(shape, F32)
        for (o, d), block in messages.items():
            for s in range(slots):
                q = jnp.broadcast_to(block[slots + s:slots + s + 1, :], shape)
                hit = q - float(d * PT_DEV) == tile
                count = count + jnp.where(hit, jnp.broadcast_to(block[s:s + 1, :], shape), 0.0)
        scale = (1.0 / jnp.sqrt(jnp.maximum(count, 1.0))).T
        for t in range(tiles_near):
            col_scale[t] = jnp.broadcast_to(scale[:, t:t + 1], (cols, lanes))

    def stage_row_scale():
        wait_all(ri_buf, ri_sem)
        total = ri_send[b]
        for o in range(1, np_):
            total = total + ri_buf[o - 1]
        row_scale[...] = wide(1.0 / jnp.sqrt(jnp.maximum(total, 1.0)), width)

    def stage_sum(turn, k):
        wait_all(rs_buf.at[k], rs_sem.at[k])
        blocks = [col_send[k, a] if o == 0 else rs_buf[k, o - 1] for o in range(nv)]
        blocks = jnp.concatenate([x.reshape(slots * part, width) for x in blocks], axis=0)
        total = jnp.dot(scatter_mat[...], halves(blocks), preferred_element_type=F32)
        total_buf[k] = total.reshape(tiles_near, part, width)
        f_copy(turn, k).start()
        b_copy(turn, k).start()

    def stage_project(layer, turn, k):
        wait_all(side_buf.at[turn, k], side_sem.at[turn, k])
        at = pl.multiple_of(k * chunk + a * part, part)
        scale = wide(col_scale[:, pl.ds(at, part), :], width)
        term = (total_buf[k] + side_buf[turn, k]) * scale
        term = term.reshape(tiles_near * part, width).astype(BF16)
        term = jnp.dot(gather_mat[...], term, preferred_element_type=F32).astype(BF16)
        chosen = jnp.dot(term, wcol_ref[layer], preferred_element_type=F32)
        chosen = chosen.reshape(nv, slots, part, width)
        ag_buf[k, 0] = chosen[0]
        for o in range(1, nv):
            ag_send[k, o - 1] = chosen[o]
            ag_copy(k, o).start()

    def stage_row_project(layer):
        wait_all(row_rs, rr_sem)
        total = row_send[b]
        for o in range(1, np_):
            total = total + row_rs[o - 1]
        term = (total * row_scale[...]).astype(BF16)
        row_ag_send[...] = (
            jnp.dot(term, wrow_ref[layer], preferred_element_type=F32)
            + bias_ref[pl.ds(layer, 1), :])
        for o in range(1, np_):
            ra_copy(o).start()

    def stage_row_collect():
        wait_all(row_ag, ra_sem)

        for j in range(np_):
            o = lax.rem(b - j + np_, np_)
            got = row_ag[jnp.maximum(o - 1, 0)]
            block = jnp.where(jnp.full(got.shape, o, jnp.int32) == 0, row_ag_send[...], got)
            at = j * share
            row_p[at // rows, at % rows:at % rows + share, :] = block

    def exchange(layer, carry):
        turn = lax.rem(layer, 2)
        for name, k in stage_order(nk):
            if name == "sum":
                stage_sum(turn, k)
            elif name == "project":
                stage_project(layer, turn, k)
            elif name == "self":
                @pl.when(layer < layers - 1)
                def _():
                    self_project(layer, k, False)

                @pl.when(layer == layers - 1)
                def _():
                    self_project(layer, k, True)
            elif name == "tables":
                pl.when(layer == 0)(stage_tables)
            elif name == "bound":
                for early in range(shifts):
                    @pl.when(layer == early)
                    def _():
                        for piece in range(2 * nk):
                            if piece % (4 * shifts) == 4 * early + k:
                                build_bound(piece // 2, piece % 2)
            else:
                pl.when(layer == 0)(stage_row_scale)
                stage_row_project(layer)
        stage_row_collect()
        for k in range(nk):
            wait_all(ag_buf.at[k, pl.ds(1, nv - 1)], ag_sem.at[k])

            @pl.when(layer < layers - 1)
            def _():
                layer_chunk(k)
                if k == nk - 1:
                    send_rows()
                send_cols(k)

            @pl.when(layer == layers - 1)
            def _():
                last_chunk(k)
        return carry

    shifts = min(layers - 1, 2)
    if shifts == 0:
        for k in range(nk):
            for half in range(2):
                build_bound(k, half)
    lax.fori_loop(0, layers, exchange, 0)


def hand_over_kernel(cur_ref, out_ref, sem):
    copies = [pltpu.make_async_copy(cur_ref.at[s], out_ref.at[s], sem.at[s])
              for s in range(cur_ref.shape[0])]
    for copy in copies:
        copy.start()
    for copy in copies:
        copy.wait()


def shards(nv, np_, features, tiles, masks, w_self, w_col, w_row, bias):
    slots, rows, cols, width = features.shape
    layers = w_self.shape[0]
    nk = max(cols // (8 * nv), 1)
    chunk = cols // nk
    part = chunk // nv
    share = VT_DEV * rows // np_
    group = 256 // chunk
    near = 3 * nv - 1
    tiles_near = 2 * PT_DEV
    vmem = pltpu.VMEM
    dma = pltpu.SemaphoreType.DMA
    whole = pl.BlockSpec(memory_space=pltpu.VMEM)
    away = pl.BlockSpec(memory_space=pltpu.HBM)
    scratch = [
        vmem(masks.shape, jnp.int32),
        vmem(w_self.shape, BF16),
        vmem(w_col.shape, BF16),
        vmem(w_row.shape, BF16),
        vmem((slots, rows, cols, width), F32),
        vmem((slots, rows, cols, min(width, 128)), BF16),
        vmem((slots, nk, rows // group, chunk + 2 * group, group * chunk), BF16),
        vmem((nv * slots * part, tiles_near * part), BF16),
        vmem((tiles_near * part, 2 * nv * slots * part), BF16),
        vmem((nk, nv, slots, part, width), F32),
        vmem((nk, nv - 1, slots, part, width), F32),
        vmem((nk, tiles_near, part, width), F32),
        vmem((2, nk, tiles_near, part, width), F32),
        vmem((nk, nv - 1, slots, part, width), F32),
        vmem((nk, nv, slots, part, width), F32),
        vmem((slots, rows, width), F32),
        vmem((np_, share, width), F32),
        vmem((np_ - 1, share, width), F32),
        vmem((share, width), F32),
        vmem((np_ - 1, share, width), F32),
        vmem((VT_DEV, rows, width), F32),
        vmem((2 * slots, cols), F32),
        vmem((near, 2 * slots, cols), F32),
        vmem((np_, share, cols), F32),
        vmem((np_ - 1, share, cols), F32),
        vmem((tiles_near, cols, cols), F32),
        vmem((share, width), F32),
        dma((nk,)),
        dma((4,)),
        dma((nk, 2)), dma((2, nk, 2)), dma((nk, 2)),
        dma((2,)), dma((2,)), dma((2,)), dma((2,)),
    ]
    current = pl.pallas_call(
        functools.partial(layers_kernel, nv, np_, nk),
        out_shape=jax.ShapeDtypeStruct(features.shape, BF16),
        in_specs=[
            pl.BlockSpec(memory_space=pltpu.SMEM),
            away, away, away, away, away, whole,
        ],
        out_specs=whole,
        scratch_shapes=scratch,
        compiler_params=pltpu.CompilerParams(
            collective_id=0, has_side_effects=True, vmem_limit_bytes=44 * 1024 * 1024),
        name="layers",
    )(*[pltpu.with_memory_space_constraint(x, pltpu.HBM)
        for x in (tiles.T, features, masks, w_self, w_col, w_row, bias)])
    return pl.pallas_call(
        hand_over_kernel,
        out_shape=jax.ShapeDtypeStruct(features.shape, BF16),
        in_specs=[pl.BlockSpec(memory_space=pl.ANY)],
        out_specs=away,
        scratch_shapes=[dma((slots,))],
        compiler_params=pltpu.CompilerParams(vmem_limit_bytes=1024 * 1024),
        name="hand_over",
    )(current)


def solution(mesh):
    in_specs = (
        P(("view", "point"), None, None, None),
        P(("view", "point"), None),
        P(("view", "point"), None, None),
        P(), P(), P(), P(),
    )
    out_specs = P(("view", "point"), None, None, None)
    body = functools.partial(shards, mesh.shape["view"], mesh.shape["point"])
    return jax.shard_map(body, mesh=mesh, in_specs=in_specs, out_specs=out_specs, check_vma=False)
```

```python
import functools

import jax
import jax.numpy as jnp
from jax import lax
from jax.experimental import pallas as pl
from jax.experimental.pallas import tpu as pltpu
from jax.sharding import PartitionSpec as P

VT_DEV = 4
PT_DEV = 4
MESH = pl.DeviceIdType.MESH
F32 = jnp.float32
BF16 = jnp.bfloat16
BIG = 2.0 ** 100


def wide(x, width):
    reps = width // x.shape[-1]
    return x if reps == 1 else jnp.concatenate([x] * reps, axis=-1)


def stage_order(nk):
    stages = []
    for k in range(nk):
        stages.append(("self", k))
        if k == 0:
            stages.append(("tables", 0))
        stages.append(("sum", k))
    stages.append(("row", 0))
    stages += [("project", k) for k in range(nk)]
    return stages + [("bound", i) for i in range(4)]


def layers_kernel(
    nv, np_, nk,
    tiles_ref, feat_ref, mask_hbm, wself_hbm, wcol_hbm, wrow_hbm, bias_ref,
    cur,
    mask_ref, wself_ref, wcol_ref, wrow_ref, self_p, bound, pick, gather_mat, scatter_mat,
    col_send, rs_buf, total_buf, side_buf, ag_send, ag_buf,
    row_acc, row_send, row_rs, row_ag_send, row_ag, row_p,
    cm_send, cm_buf, ri_send, ri_buf, col_scale, row_scale,
    feat_sem, in_sem, rs_sem, side_sem, ag_sem, rr_sem, ra_sem, cm_sem, ri_sem,
):
    a = lax.axis_index("view")
    b = lax.axis_index("point")
    slots, rows, cols, width = cur.shape
    layers = wself_ref.shape[0]
    chunk = cols // nk
    part = chunk // nv
    share = row_send.shape[1]
    tiles_near = 2 * PT_DEV

    def view_at(o):
        return lax.rem(a + o, nv)

    def point_at(o):
        return lax.rem(b + o + np_, np_)

    def remote(src, dst, sems, va, pb):
        return pltpu.make_async_remote_copy(
            src_ref=src, dst_ref=dst, send_sem=sems.at[0], recv_sem=sems.at[1],
            device_id=(va, pb), device_id_type=MESH,
        )

    def wait_all(landed, sems):
        for end in range(2):
            pltpu.make_async_copy(landed, landed, sems.at[end]).wait()

    def rs_copy(k, o):
        return remote(col_send.at[k, view_at(o)], rs_buf.at[k, o - 1],
                      rs_sem.at[k], view_at(o), b)

    def ag_copy(k, o):
        return remote(ag_send.at[k, o - 1], ag_buf.at[k, o],
                      ag_sem.at[k], view_at(o), b)

    def f_copy(turn, k):
        return remote(total_buf.at[k, pl.ds(PT_DEV, PT_DEV)], side_buf.at[turn, k, pl.ds(0, PT_DEV)],
                      side_sem.at[turn, k], a, point_at(1))

    def b_copy(turn, k):
        return remote(total_buf.at[k, pl.ds(0, PT_DEV)], side_buf.at[turn, k, pl.ds(PT_DEV, PT_DEV)],
                      side_sem.at[turn, k], a, point_at(-1))

    def rr_copy(o):
        return remote(row_send.at[point_at(o)], row_rs.at[o - 1],
                      rr_sem, a, point_at(o))

    def ra_copy(o):
        return remote(row_ag_send, row_ag.at[o - 1], ra_sem, a, point_at(o))

    near = [(o, d) for d in (0, 1, -1) for o in range(nv) if (o, d) != (0, 0)]

    def cm_copy(n):
        o, d = near[n]
        return remote(cm_send, cm_buf.at[n], cm_sem, view_at(o), point_at(d))

    def ri_copy(o):
        return remote(ri_send.at[point_at(o)], ri_buf.at[o - 1],
                      ri_sem, a, point_at(o))

    def feat_copy(k):
        span = pl.ds(k * chunk, chunk)
        return pltpu.make_async_copy(
            feat_ref.at[:, :, span, :], cur.at[:, :, span, :], feat_sem.at[k])

    def in_copy(n):
        src = (mask_hbm, wself_hbm, wcol_hbm, wrow_hbm)[n]
        dst = (mask_ref, wself_ref, wcol_ref, wrow_ref)[n]
        return pltpu.make_async_copy(src, dst, in_sem.at[n])

    in_copy(0).start()
    for k in range(nk):
        feat_copy(k).start()
    for n in range(1, 4):
        in_copy(n).start()

    barrier = pltpu.get_barrier_semaphore()
    friends = [(0, o) for o in range(2, np_ - 1)] + near
    for o, d in friends:
        pl.semaphore_signal(barrier, inc=1, device_id=(view_at(o), point_at(d)) if (o, d) in near
                            else (a, point_at(d)), device_id_type=MESH)
    in_copy(0).wait()

    group = pick.shape[4] // chunk
    lanes = cols

    for s in range(slots):
        cm_send[s:s + 1, :] = jnp.sum(mask_ref[s].astype(F32), axis=0, keepdims=True)
        cm_send[slots + s:slots + s + 1, :] = jnp.full(
            (1, lanes), tiles_ref[1, s], jnp.int32).astype(F32)
    for v in range(VT_DEV):
        total = jnp.zeros((rows, lanes), F32)
        for s in range(slots):
            rcount = jnp.broadcast_to(
                jnp.sum(mask_ref[s].astype(F32), axis=1, keepdims=True), (rows, lanes))
            hit = jnp.full((rows, lanes), tiles_ref[0, s], jnp.int32) == v
            total = total + jnp.where(hit, rcount, 0.0)
        for i in range(max(rows // share, 1)):
            at = v * rows + i * share
            ri_send[at // share] = total[i * share:(i + 1) * share]

    def build_pick(s, carry):
        shape = (group, group * chunk)
        lane = lax.broadcasted_iota(jnp.int32, shape, 1)
        of_view = lane // chunk == lax.broadcasted_iota(jnp.int32, shape, 0)
        shape = (chunk, group * chunk)
        lane = lax.broadcasted_iota(jnp.int32, shape, 1)
        of_point = lane % chunk == lax.broadcasted_iota(jnp.int32, shape, 0)
        for g in range(rows // group):
            m = mask_ref[s, g * group:(g + 1) * group, :].astype(F32)
            for k in range(nk):
                tiled = jnp.concatenate([m[:, k * chunk:(k + 1) * chunk]] * group, axis=1)
                by_view = jnp.where(of_view, tiled, 0.0)
                flat = jnp.sum(by_view, axis=0, keepdims=True)
                by_point = jnp.where(of_point, jnp.broadcast_to(flat, shape), 0.0)
                both = jnp.concatenate([by_point, by_view, jnp.ones_like(by_view)], axis=0)
                pick[s, k, g] = both.astype(BF16)
        return carry

    lax.fori_loop(0, slots, build_pick, 0)

    def sum_rows(k, s, value_of):
        col = jnp.zeros((chunk, width), F32)
        for g in range(rows // group):
            both = jnp.dot(pick[s, k, g], value_of(g), preferred_element_type=F32)
            col = col + both[:chunk]
            new = both[chunk:chunk + group]
            at = pl.ds(g * group, group)
            if k == 0:
                row_acc[s, at, :] = new
            else:
                row_acc[s, at, :] = row_acc[s, at, :] + new
        for j in range(nv):
            col_send[k, j, s] = col[j * part:(j + 1) * part]

    def entries(k, s, g):
        span = pl.ds(k * chunk, chunk)
        return cur[s, g * group:(g + 1) * group, span, :].reshape(group * chunk, width)

    def over_slots(slot):
        lax.fori_loop(0, slots, slot, 0, unroll=4 if slots % 4 == 0 else 1)

    def first_sums(k):
        def slot(s, carry):
            sum_rows(k, s, lambda g: entries(k, s, g))
            return carry
        over_slots(slot)

    def build_bound(k, half):
        shape = (2 * group, bound.shape[3])
        row = lax.broadcasted_iota(jnp.int32, shape, 0)
        ends = jnp.where(row < group, 2.0 * BIG, jnp.where(row == group, -BIG, 0.0)).astype(BF16)

        def slot(s, carry):
            for g in range(rows // group):
                x = lax.dot_general(
                    pick[s, k, g, chunk:, :], ends, (((0,), (0,)), ((), ())),
                    preferred_element_type=F32)
                bound[s, g * group:(g + 1) * group, pl.ds(k * chunk, chunk), :] = (
                    x.reshape(group, chunk, shape[1]).astype(BF16))
            return carry
        lax.fori_loop(half * slots // 2, (half + 1) * slots // 2, slot, 0, unroll=True)

    def self_project(layer, k, masked):
        span = pl.ds(k * chunk, chunk)

        def slot(s, carry):
            for g in range(rows // group):
                z = jnp.dot(entries(k, s, g), wself_ref[layer], preferred_element_type=F32)
                z = z.reshape(group, chunk, width)
                if masked:
                    z = jnp.minimum(z, wide(
                        bound[s, g * group:(g + 1) * group, span, :].astype(F32), width))
                self_p[s, g * group:(g + 1) * group, span, :] = z
            return carry
        over_slots(slot)

    def mix(k, s, g):
        span = pl.ds(k * chunk, chunk)
        v = tiles_ref[0, s]
        colp = jnp.concatenate(
            [ag_buf[k, lax.rem(a - j + nv, nv), s] for j in range(nv)], axis=0)
        found = []
        for r in range(g * group, (g + 1) * group):
            rowp = jnp.broadcast_to(row_p[v, r:r + 1, :], (chunk, width))
            y = jnp.maximum((self_p[s, r, span, :] + colp + rowp).astype(BF16), 0)
            cur[s, r, span, :] = y
            found.append(y)
        return jnp.concatenate(found, axis=0)

    def layer_chunk(k):
        def slot(s, carry):
            sum_rows(k, s, lambda g: mix(k, s, g))
            return carry
        over_slots(slot)

    def last_chunk(k):
        def slot(s, carry):
            for g in range(rows // group):
                mix(k, s, g)
            return carry
        over_slots(slot)

    def send_rows():
        for v in range(VT_DEV):
            total = jnp.zeros((rows, width), F32)
            for s in range(slots):
                hit = jnp.full((rows, width), tiles_ref[0, s], jnp.int32) == v
                total = total + jnp.where(hit, row_acc[s], 0.0)
            for i in range(max(rows // share, 1)):
                at = v * rows + i * share
                row_send[at // share] = total[i * share:(i + 1) * share]
        for o in range(1, np_):
            rr_copy(o).start()

    def send_cols(k):
        for o in range(1, nv):
            rs_copy(k, o).start()

    def halves(x):
        high = x.astype(BF16)
        return jnp.concatenate([high, (x - high.astype(F32)).astype(BF16)], axis=0)

    for k in range(nk):
        feat_copy(k).wait()
        first_sums(k)
        if k == 0:
            pl.semaphore_wait(barrier, len(friends))
            for n in range(len(near)):
                cm_copy(n).start()
            for o in range(1, np_):
                ri_copy(o).start()
        if k == nk - 1:
            send_rows()
        send_cols(k)
    for n in range(1, 4):
        in_copy(n).wait()

    def stage_tables():
        wait_all(cm_buf, cm_sem)
        messages = {(0, 0): cm_send[...]}
        for n, at in enumerate(near):
            messages[at] = cm_buf[n]

        def tile_of(o, s):
            return messages[o, 0][slots + s:slots + s + 1, :]

        def lane_tiled(x, size):
            return x[:, :size] if size <= lanes else jnp.concatenate([x] * (size // lanes), axis=1)

        shape = scatter_mat.shape
        lane = lax.broadcasted_iota(jnp.int32, (1, shape[1]), 1) % (nv * slots * part)
        q_lane = jnp.zeros((1, shape[1]), F32)
        for o in range(nv):
            for s in range(slots):
                q_lane = jnp.where(lane // part == o * slots + s, lane_tiled(tile_of(o, s), shape[1]), q_lane)
        row = lax.broadcasted_iota(jnp.int32, shape, 0)
        lane = lax.broadcasted_iota(jnp.int32, shape, 1)
        hit = (jnp.broadcast_to(q_lane, shape) == (row // part).astype(F32)) & (row % part == lane % part)
        scatter_mat[...] = jnp.where(hit, 1.0, 0.0).astype(BF16)

        shape = (part, tiles_near * part)
        lane = lax.broadcasted_iota(jnp.int32, shape, 1)
        same = lane % part == lax.broadcasted_iota(jnp.int32, shape, 0)
        tile = (lane // part).astype(F32)
        found = []
        for o in range(nv):
            for s in range(slots):
                q = jnp.broadcast_to(lane_tiled(tile_of((nv - o) % nv, s), shape[1]), shape)
                found.append(jnp.where((q == tile) & same, 1.0, 0.0))
        gather_mat[...] = jnp.concatenate(found, axis=0).astype(BF16)

        shape = (tiles_near, lanes)
        tile = lax.broadcasted_iota(jnp.int32, shape, 0).astype(F32)
        count = jnp.zeros(shape, F32)
        for (o, d), block in messages.items():
            for s in range(slots):
                q = jnp.broadcast_to(block[slots + s:slots + s + 1, :], shape)
                hit = q - float(d * PT_DEV) == tile
                count = count + jnp.where(hit, jnp.broadcast_to(block[s:s + 1, :], shape), 0.0)
        scale = (1.0 / jnp.sqrt(jnp.maximum(count, 1.0))).T
        for t in range(tiles_near):
            col_scale[t] = jnp.broadcast_to(scale[:, t:t + 1], (cols, lanes))

    def stage_row_scale():
        wait_all(ri_buf, ri_sem)
        total = ri_send[b]
        for o in range(1, np_):
            total = total + ri_buf[o - 1]
        row_scale[...] = wide(1.0 / jnp.sqrt(jnp.maximum(total, 1.0)), width)

    def stage_sum(turn, k):
        wait_all(rs_buf.at[k], rs_sem.at[k])
        blocks = [col_send[k, a] if o == 0 else rs_buf[k, o - 1] for o in range(nv)]
        blocks = jnp.concatenate([x.reshape(slots * part, width) for x in blocks], axis=0)
        total = jnp.dot(scatter_mat[...], halves(blocks), preferred_element_type=F32)
        total_buf[k] = total.reshape(tiles_near, part, width)
        f_copy(turn, k).start()
        b_copy(turn, k).start()

    def stage_project(layer, turn, k):
        wait_all(side_buf.at[turn, k], side_sem.at[turn, k])
        at = pl.multiple_of(k * chunk + a * part, part)
        scale = wide(col_scale[:, pl.ds(at, part), :], width)
        term = (total_buf[k] + side_buf[turn, k]) * scale
        term = term.reshape(tiles_near * part, width).astype(BF16)
        term = jnp.dot(gather_mat[...], term, preferred_element_type=F32).astype(BF16)
        chosen = jnp.dot(term, wcol_ref[layer], preferred_element_type=F32)
        chosen = chosen.reshape(nv, slots, part, width)
        ag_buf[k, 0] = chosen[0]
        for o in range(1, nv):
            ag_send[k, o - 1] = chosen[o]
            ag_copy(k, o).start()

    def stage_row_project(layer):
        wait_all(row_rs, rr_sem)
        total = row_send[b]
        for o in range(1, np_):
            total = total + row_rs[o - 1]
        term = (total * row_scale[...]).astype(BF16)
        row_ag_send[...] = (
            jnp.dot(term, wrow_ref[layer], preferred_element_type=F32)
            + bias_ref[pl.ds(layer, 1), :])
        for o in range(1, np_):
            ra_copy(o).start()

    def stage_row_collect():
        wait_all(row_ag, ra_sem)

        for j in range(np_):
            o = lax.rem(b - j + np_, np_)
            got = row_ag[jnp.maximum(o - 1, 0)]
            block = jnp.where(jnp.full(got.shape, o, jnp.int32) == 0, row_ag_send[...], got)
            at = j * share
            row_p[at // rows, at % rows:at % rows + share, :] = block

    def exchange(layer, carry):
        turn = lax.rem(layer, 2)
        for name, k in stage_order(nk):
            if name == "sum":
                stage_sum(turn, k)
            elif name == "project":
                stage_project(layer, turn, k)
            elif name == "self":
                @pl.when(layer < layers - 1)
                def _():
                    self_project(layer, k, False)

                @pl.when(layer == layers - 1)
                def _():
                    self_project(layer, k, True)
            elif name == "tables":
                pl.when(layer == 0)(stage_tables)
            elif name == "bound":
                for early in range(shifts):
                    @pl.when(layer == early)
                    def _():
                        for piece in range(2 * nk):
                            if piece % (4 * shifts) == 4 * early + k:
                                build_bound(piece // 2, piece % 2)
            else:
                pl.when(layer == 0)(stage_row_scale)
                stage_row_project(layer)
        stage_row_collect()
        for k in range(nk):
            wait_all(ag_buf.at[k, pl.ds(1, nv - 1)], ag_sem.at[k])

            @pl.when(layer < layers - 1)
            def _():
                layer_chunk(k)
                if k == nk - 1:
                    send_rows()
                send_cols(k)

            @pl.when(layer == layers - 1)
            def _():
                last_chunk(k)
        return carry

    shifts = min(layers - 1, 2)
    if shifts == 0:
        for k in range(nk):
            for half in range(2):
                build_bound(k, half)
    lax.fori_loop(0, layers, exchange, 0)


def hand_over_kernel(cur_ref, out_ref, sem):
    copies = [pltpu.make_async_copy(cur_ref.at[s], out_ref.at[s], sem.at[s])
              for s in range(cur_ref.shape[0])]
    for copy in copies:
        copy.start()
    for copy in copies:
        copy.wait()


def shards(nv, np_, features, tiles, masks, w_self, w_col, w_row, bias):
    slots, rows, cols, width = features.shape
    layers = w_self.shape[0]
    nk = max(cols // (8 * nv), 1)
    chunk = cols // nk
    part = chunk // nv
    share = VT_DEV * rows // np_
    group = 256 // chunk
    near = 3 * nv - 1
    tiles_near = 2 * PT_DEV
    vmem = pltpu.VMEM
    dma = pltpu.SemaphoreType.DMA
    whole = pl.BlockSpec(memory_space=pltpu.VMEM)
    away = pl.BlockSpec(memory_space=pltpu.HBM)
    scratch = [
        vmem(masks.shape, jnp.int32),
        vmem(w_self.shape, BF16),
        vmem(w_col.shape, BF16),
        vmem(w_row.shape, BF16),
        vmem((slots, rows, cols, width), F32),
        vmem((slots, rows, cols, min(width, 128)), BF16),
        vmem((slots, nk, rows // group, chunk + 2 * group, group * chunk), BF16),
        vmem((nv * slots * part, tiles_near * part), BF16),
        vmem((tiles_near * part, 2 * nv * slots * part), BF16),
        vmem((nk, nv, slots, part, width), F32),
        vmem((nk, nv - 1, slots, part, width), F32),
        vmem((nk, tiles_near, part, width), F32),
        vmem((2, nk, tiles_near, part, width), F32),
        vmem((nk, nv - 1, slots, part, width), F32),
        vmem((nk, nv, slots, part, width), F32),
        vmem((slots, rows, width), F32),
        vmem((np_, share, width), F32),
        vmem((np_ - 1, share, width), F32),
        vmem((share, width), F32),
        vmem((np_ - 1, share, width), F32),
        vmem((VT_DEV, rows, width), F32),
        vmem((2 * slots, cols), F32),
        vmem((near, 2 * slots, cols), F32),
        vmem((np_, share, cols), F32),
        vmem((np_ - 1, share, cols), F32),
        vmem((tiles_near, cols, cols), F32),
        vmem((share, width), F32),
        dma((nk,)),
        dma((4,)),
        dma((nk, 2)), dma((2, nk, 2)), dma((nk, 2)),
        dma((2,)), dma((2,)), dma((2,)), dma((2,)),
    ]
    current = pl.pallas_call(
        functools.partial(layers_kernel, nv, np_, nk),
        out_shape=jax.ShapeDtypeStruct(features.shape, BF16),
        in_specs=[
            pl.BlockSpec(memory_space=pltpu.SMEM),
            away, away, away, away, away, whole,
        ],
        out_specs=whole,
        scratch_shapes=scratch,
        compiler_params=pltpu.CompilerParams(
            collective_id=0, has_side_effects=True, vmem_limit_bytes=44 * 1024 * 1024),
        name="layers",
    )(*[pltpu.with_memory_space_constraint(x, pltpu.HBM)
        for x in (tiles.T, features, masks, w_self, w_col, w_row, bias)])
    return pl.pallas_call(
        hand_over_kernel,
        out_shape=jax.ShapeDtypeStruct(features.shape, BF16),
        in_specs=[pl.BlockSpec(memory_space=pl.ANY)],
        out_specs=away,
        scratch_shapes=[dma((slots,))],
        compiler_params=pltpu.CompilerParams(vmem_limit_bytes=1024 * 1024),
        name="hand_over",
    )(current)


def solution(mesh):
    in_specs = (
        P(("view", "point"), None, None, None),
        P(("view", "point"), None),
        P(("view", "point"), None, None),
        P(), P(), P(), P(),
    )
    out_specs = P(("view", "point"), None, None, None)
    body = functools.partial(shards, mesh.shape["view"], mesh.shape["point"])
    return jax.shard_map(body, mesh=mesh, in_specs=in_specs, out_specs=out_specs, check_vma=False)
```

```python
import functools

import jax
import jax.numpy as jnp
from jax import lax
from jax.experimental import pallas as pl
from jax.experimental.pallas import tpu as pltpu
from jax.sharding import PartitionSpec as P

VT_DEV = 4
PT_DEV = 4
MESH = pl.DeviceIdType.MESH
F32 = jnp.float32
BF16 = jnp.bfloat16
BIG = 2.0 ** 100


def wide(x, width):
    reps = width // x.shape[-1]
    return x if reps == 1 else jnp.concatenate([x] * reps, axis=-1)


def paired(me, o, size):
    if size & (size - 1):
        return lax.rem(me + o, size)
    total = me * 0
    bit = 1
    while bit < size:
        mine = lax.rem(me // bit, 2)
        total = total + bit * (1 - mine if o & bit else mine)
        bit *= 2
    return total


def step_of(me, other, size):
    if size & (size - 1):
        return lax.rem(me - other + size, size)
    return paired(me, other, size)


def stage_order(nk):
    stages = []
    for k in range(nk):
        stages.append(("self", k))
        if k == 0:
            stages.append(("tables", 0))
        stages.append(("sum", k))
    stages.append(("row", 0))
    stages += [("project", k) for k in range(nk)]
    return stages + [("bound", i) for i in range(4)]


def layers_kernel(
    nv, np_, nk,
    tiles_ref, feat_ref, mask_hbm, wself_hbm, wcol_hbm, wrow_hbm, bias_ref,
    cur,
    mask_ref, wself_ref, wcol_ref, wrow_ref, self_p, bound, pick, gather_mat, scatter_mat,
    col_send, rs_buf, total_buf, side_buf, ag_send, ag_buf,
    row_acc, row_send, row_rs, row_ag_send, row_ag, row_p,
    cm_send, cm_buf, ri_send, ri_buf, col_scale, row_scale,
    feat_sem, in_sem, rs_sem, side_sem, ag_sem, rr_sem, ra_sem, cm_sem, ri_sem,
):
    a = lax.axis_index("view")
    b = lax.axis_index("point")
    slots, rows, cols, width = cur.shape
    layers = wself_ref.shape[0]
    chunk = cols // nk
    part = chunk // nv
    share = row_send.shape[1]
    tiles_near = 2 * PT_DEV

    def view_at(o):
        return paired(a, o, nv)

    def fellow_at(o):
        return paired(b, o, np_)

    def point_at(o):
        return lax.rem(b + o + np_, np_)

    def remote(src, dst, sems, va, pb):
        return pltpu.make_async_remote_copy(
            src_ref=src, dst_ref=dst, send_sem=sems.at[0], recv_sem=sems.at[1],
            device_id=(va, pb), device_id_type=MESH,
        )

    def wait_all(landed, sems):
        for end in range(2):
            pltpu.make_async_copy(landed, landed, sems.at[end]).wait()

    def rs_copy(k, o):
        return remote(col_send.at[k, view_at(o)], rs_buf.at[k, o - 1],
                      rs_sem.at[k], view_at(o), b)

    def ag_copy(k, o):
        return remote(ag_send.at[k, o - 1], ag_buf.at[k, o],
                      ag_sem.at[k], view_at(o), b)

    def f_copy(turn, k):
        return remote(total_buf.at[k, pl.ds(PT_DEV, PT_DEV)], side_buf.at[turn, k, pl.ds(0, PT_DEV)],
                      side_sem.at[turn, k], a, point_at(1))

    def b_copy(turn, k):
        return remote(total_buf.at[k, pl.ds(0, PT_DEV)], side_buf.at[turn, k, pl.ds(PT_DEV, PT_DEV)],
                      side_sem.at[turn, k], a, point_at(-1))

    def rr_copy(o):
        return remote(row_send.at[fellow_at(o)], row_rs.at[o - 1],
                      rr_sem, a, fellow_at(o))

    def ra_copy(o):
        return remote(row_ag_send, row_ag.at[o - 1], ra_sem, a, fellow_at(o))

    near = [(o, d) for d in (0, 1, -1) for o in range(nv) if (o, d) != (0, 0)]

    def cm_copy(n):
        o, d = near[n]
        return remote(cm_send, cm_buf.at[n], cm_sem, view_at(o), point_at(d))

    def ri_copy(o):
        return remote(ri_send.at[fellow_at(o)], ri_buf.at[o - 1],
                      ri_sem, a, fellow_at(o))

    def feat_copy(k):
        span = pl.ds(k * chunk, chunk)
        return pltpu.make_async_copy(
            feat_ref.at[:, :, span, :], cur.at[:, :, span, :], feat_sem.at[k])

    def in_copy(n):
        src = (mask_hbm, wself_hbm, wcol_hbm, wrow_hbm)[n]
        dst = (mask_ref, wself_ref, wcol_ref, wrow_ref)[n]
        return pltpu.make_async_copy(src, dst, in_sem.at[n])

    in_copy(0).start()
    for k in range(nk):
        feat_copy(k).start()
    for n in range(1, 4):
        in_copy(n).start()

    barrier = pltpu.get_barrier_semaphore()
    friends = [(0, o) for o in range(2, np_ - 1)] + near
    for o, d in friends:
        pl.semaphore_signal(barrier, inc=1, device_id=(view_at(o), point_at(d)) if (o, d) in near
                            else (a, point_at(d)), device_id_type=MESH)
    in_copy(0).wait()

    group = pick.shape[4] // chunk
    lanes = cols

    for s in range(slots):
        cm_send[s:s + 1, :] = jnp.sum(mask_ref[s].astype(F32), axis=0, keepdims=True)
        cm_send[slots + s:slots + s + 1, :] = jnp.full(
            (1, lanes), tiles_ref[1, s], jnp.int32).astype(F32)
    for v in range(VT_DEV):
        total = jnp.zeros((rows, lanes), F32)
        for s in range(slots):
            rcount = jnp.broadcast_to(
                jnp.sum(mask_ref[s].astype(F32), axis=1, keepdims=True), (rows, lanes))
            hit = jnp.full((rows, lanes), tiles_ref[0, s], jnp.int32) == v
            total = total + jnp.where(hit, rcount, 0.0)
        for i in range(max(rows // share, 1)):
            at = v * rows + i * share
            ri_send[at // share] = total[i * share:(i + 1) * share]

    def build_pick(s, carry):
        shape = (group, group * chunk)
        lane = lax.broadcasted_iota(jnp.int32, shape, 1)
        of_view = lane // chunk == lax.broadcasted_iota(jnp.int32, shape, 0)
        shape = (chunk, group * chunk)
        lane = lax.broadcasted_iota(jnp.int32, shape, 1)
        of_point = lane % chunk == lax.broadcasted_iota(jnp.int32, shape, 0)
        for g in range(rows // group):
            m = mask_ref[s, g * group:(g + 1) * group, :].astype(F32)
            for k in range(nk):
                tiled = jnp.concatenate([m[:, k * chunk:(k + 1) * chunk]] * group, axis=1)
                by_view = jnp.where(of_view, tiled, 0.0)
                flat = jnp.sum(by_view, axis=0, keepdims=True)
                by_point = jnp.where(of_point, jnp.broadcast_to(flat, shape), 0.0)
                both = jnp.concatenate([by_point, by_view, jnp.ones_like(by_view)], axis=0)
                pick[s, k, g] = both.astype(BF16)
        return carry

    lax.fori_loop(0, slots, build_pick, 0)

    def sum_rows(k, s, value_of):
        col = jnp.zeros((chunk, width), F32)
        for g in range(rows // group):
            both = jnp.dot(pick[s, k, g], value_of(g), preferred_element_type=F32)
            col = col + both[:chunk]
            new = both[chunk:chunk + group]
            at = pl.ds(g * group, group)
            if k == 0:
                row_acc[s, at, :] = new
            else:
                row_acc[s, at, :] = row_acc[s, at, :] + new
        for j in range(nv):
            col_send[k, j, s] = col[j * part:(j + 1) * part]

    def entries(k, s, g):
        span = pl.ds(k * chunk, chunk)
        return cur[s, g * group:(g + 1) * group, span, :].reshape(group * chunk, width)

    def over_slots(slot):
        lax.fori_loop(0, slots, slot, 0, unroll=4 if slots % 4 == 0 else 1)

    def first_sums(k):
        def slot(s, carry):
            sum_rows(k, s, lambda g: entries(k, s, g))
            return carry
        over_slots(slot)

    def build_bound(k, half):
        shape = (2 * group, bound.shape[3])
        row = lax.broadcasted_iota(jnp.int32, shape, 0)
        ends = jnp.where(row < group, 2.0 * BIG, jnp.where(row == group, -BIG, 0.0)).astype(BF16)

        def slot(s, carry):
            for g in range(rows // group):
                x = lax.dot_general(
                    pick[s, k, g, chunk:, :], ends, (((0,), (0,)), ((), ())),
                    preferred_element_type=F32)
                bound[s, g * group:(g + 1) * group, pl.ds(k * chunk, chunk), :] = (
                    x.reshape(group, chunk, shape[1]).astype(BF16))
            return carry
        lax.fori_loop(half * slots // 2, (half + 1) * slots // 2, slot, 0, unroll=True)

    def self_project(layer, k, masked):
        span = pl.ds(k * chunk, chunk)

        def slot(s, carry):
            for g in range(rows // group):
                z = jnp.dot(entries(k, s, g), wself_ref[layer], preferred_element_type=F32)
                z = z.reshape(group, chunk, width)
                if masked:
                    z = jnp.minimum(z, wide(
                        bound[s, g * group:(g + 1) * group, span, :].astype(F32), width))
                self_p[s, g * group:(g + 1) * group, span, :] = z
            return carry
        over_slots(slot)

    def mix(k, s, g):
        span = pl.ds(k * chunk, chunk)
        v = tiles_ref[0, s]
        colp = jnp.concatenate(
            [ag_buf[k, step_of(a, j, nv), s] for j in range(nv)], axis=0)
        found = []
        for r in range(g * group, (g + 1) * group):
            rowp = jnp.broadcast_to(row_p[v, r:r + 1, :], (chunk, width))
            y = jnp.maximum((self_p[s, r, span, :] + colp + rowp).astype(BF16), 0)
            cur[s, r, span, :] = y
            found.append(y)
        return jnp.concatenate(found, axis=0)

    def layer_chunk(k):
        def slot(s, carry):
            sum_rows(k, s, lambda g: mix(k, s, g))
            return carry
        over_slots(slot)

    def last_chunk(k):
        def slot(s, carry):
            for g in range(rows // group):
                mix(k, s, g)
            return carry
        over_slots(slot)

    def send_rows():
        for v in range(VT_DEV):
            total = jnp.zeros((rows, width), F32)
            for s in range(slots):
                hit = jnp.full((rows, width), tiles_ref[0, s], jnp.int32) == v
                total = total + jnp.where(hit, row_acc[s], 0.0)
            for i in range(max(rows // share, 1)):
                at = v * rows + i * share
                row_send[at // share] = total[i * share:(i + 1) * share]
        for o in reversed(range(1, np_)):
            rr_copy(o).start()

    def send_cols(k):
        for o in reversed(range(1, nv)):
            rs_copy(k, o).start()

    def halves(x):
        high = x.astype(BF16)
        return jnp.concatenate([high, (x - high.astype(F32)).astype(BF16)], axis=0)

    for k in range(nk):
        feat_copy(k).wait()
        first_sums(k)
        if k == 0:
            pl.semaphore_wait(barrier, len(friends))
            for n in range(len(near)):
                cm_copy(n).start()
            for o in range(1, np_):
                ri_copy(o).start()
        if k == nk - 1:
            send_rows()
        send_cols(k)
    for n in range(1, 4):
        in_copy(n).wait()

    def stage_tables():
        wait_all(cm_buf, cm_sem)
        messages = {(0, 0): cm_send[...]}
        for n, at in enumerate(near):
            messages[at] = cm_buf[n]

        def tile_of(o, s):
            return messages[o, 0][slots + s:slots + s + 1, :]

        def lane_tiled(x, size):
            return x[:, :size] if size <= lanes else jnp.concatenate([x] * (size // lanes), axis=1)

        shape = scatter_mat.shape
        lane = lax.broadcasted_iota(jnp.int32, (1, shape[1]), 1) % (nv * slots * part)
        q_lane = jnp.zeros((1, shape[1]), F32)
        for o in range(nv):
            for s in range(slots):
                q_lane = jnp.where(lane // part == o * slots + s, lane_tiled(tile_of(o, s), shape[1]), q_lane)
        row = lax.broadcasted_iota(jnp.int32, shape, 0)
        lane = lax.broadcasted_iota(jnp.int32, shape, 1)
        hit = (jnp.broadcast_to(q_lane, shape) == (row // part).astype(F32)) & (row % part == lane % part)
        scatter_mat[...] = jnp.where(hit, 1.0, 0.0).astype(BF16)

        shape = (part, tiles_near * part)
        lane = lax.broadcasted_iota(jnp.int32, shape, 1)
        same = lane % part == lax.broadcasted_iota(jnp.int32, shape, 0)
        tile = (lane // part).astype(F32)
        found = []
        for o in range(nv):
            for s in range(slots):
                q = jnp.broadcast_to(lane_tiled(tile_of((nv - o) % nv if nv & (nv - 1) else o, s), shape[1]), shape)
                found.append(jnp.where((q == tile) & same, 1.0, 0.0))
        gather_mat[...] = jnp.concatenate(found, axis=0).astype(BF16)

        shape = (tiles_near, lanes)
        tile = lax.broadcasted_iota(jnp.int32, shape, 0).astype(F32)
        count = jnp.zeros(shape, F32)
        for (o, d), block in messages.items():
            for s in range(slots):
                q = jnp.broadcast_to(block[slots + s:slots + s + 1, :], shape)
                hit = q - float(d * PT_DEV) == tile
                count = count + jnp.where(hit, jnp.broadcast_to(block[s:s + 1, :], shape), 0.0)
        scale = (1.0 / jnp.sqrt(jnp.maximum(count, 1.0))).T
        for t in range(tiles_near):
            col_scale[t] = jnp.broadcast_to(scale[:, t:t + 1], (cols, lanes))

    def stage_row_scale():
        wait_all(ri_buf, ri_sem)
        total = ri_send[b]
        for o in range(1, np_):
            total = total + ri_buf[o - 1]
        row_scale[...] = wide(1.0 / jnp.sqrt(jnp.maximum(total, 1.0)), width)

    def stage_sum(turn, k):
        wait_all(rs_buf.at[k], rs_sem.at[k])
        blocks = [col_send[k, a] if o == 0 else rs_buf[k, o - 1] for o in range(nv)]
        blocks = jnp.concatenate([x.reshape(slots * part, width) for x in blocks], axis=0)
        total = jnp.dot(scatter_mat[...], halves(blocks), preferred_element_type=F32)
        total_buf[k] = total.reshape(tiles_near, part, width)
        f_copy(turn, k).start()
        b_copy(turn, k).start()

    def stage_project(layer, turn, k):
        wait_all(side_buf.at[turn, k], side_sem.at[turn, k])
        at = pl.multiple_of(k * chunk + a * part, part)
        scale = wide(col_scale[:, pl.ds(at, part), :], width)
        term = (total_buf[k] + side_buf[turn, k]) * scale
        term = term.reshape(tiles_near * part, width).astype(BF16)
        term = jnp.dot(gather_mat[...], term, preferred_element_type=F32).astype(BF16)
        chosen = jnp.dot(term, wcol_ref[layer], preferred_element_type=F32)
        chosen = chosen.reshape(nv, slots, part, width)
        ag_buf[k, 0] = chosen[0]
        for o in reversed(range(1, nv)):
            ag_send[k, o - 1] = chosen[o]
            ag_copy(k, o).start()

    def stage_row_project(layer):
        wait_all(row_rs, rr_sem)
        total = row_send[b]
        for o in range(1, np_):
            total = total + row_rs[o - 1]
        term = (total * row_scale[...]).astype(BF16)
        row_ag_send[...] = (
            jnp.dot(term, wrow_ref[layer], preferred_element_type=F32)
            + bias_ref[pl.ds(layer, 1), :])
        for o in reversed(range(1, np_)):
            ra_copy(o).start()

    def stage_row_collect():
        wait_all(row_ag, ra_sem)

        for j in range(np_):
            o = step_of(b, j, np_)
            got = row_ag[jnp.maximum(o - 1, 0)]
            block = jnp.where(jnp.full(got.shape, o, jnp.int32) == 0, row_ag_send[...], got)
            at = j * share
            row_p[at // rows, at % rows:at % rows + share, :] = block

    def exchange(layer, carry):
        turn = lax.rem(layer, 2)
        for name, k in stage_order(nk):
            if name == "sum":
                stage_sum(turn, k)
            elif name == "project":
                stage_project(layer, turn, k)
            elif name == "self":
                @pl.when(layer < layers - 1)
                def _():
                    self_project(layer, k, False)

                @pl.when(layer == layers - 1)
                def _():
                    self_project(layer, k, True)
            elif name == "tables":
                pl.when(layer == 0)(stage_tables)
            elif name == "bound":
                for early in range(shifts):
                    @pl.when(layer == early)
                    def _():
                        for piece in range(2 * nk):
                            if piece % (4 * shifts) == 4 * early + k:
                                build_bound(piece // 2, piece % 2)
            else:
                pl.when(layer == 0)(stage_row_scale)
                stage_row_project(layer)
        stage_row_collect()
        for k in range(nk):
            wait_all(ag_buf.at[k, pl.ds(1, nv - 1)], ag_sem.at[k])

            @pl.when(layer < layers - 1)
            def _():
                layer_chunk(k)
                if k == nk - 1:
                    send_rows()
                send_cols(k)

            @pl.when(layer == layers - 1)
            def _():
                last_chunk(k)
        return carry

    shifts = min(layers - 1, 2)
    if shifts == 0:
        for k in range(nk):
            for half in range(2):
                build_bound(k, half)
    lax.fori_loop(0, layers, exchange, 0)


def hand_over_kernel(cur_ref, out_ref, sem):
    copies = [pltpu.make_async_copy(cur_ref.at[s], out_ref.at[s], sem.at[s])
              for s in range(cur_ref.shape[0])]
    for copy in copies:
        copy.start()
    for copy in copies:
        copy.wait()


def shards(nv, np_, features, tiles, masks, w_self, w_col, w_row, bias):
    slots, rows, cols, width = features.shape
    layers = w_self.shape[0]
    nk = max(cols // (8 * nv), 1)
    chunk = cols // nk
    part = chunk // nv
    share = VT_DEV * rows // np_
    group = 256 // chunk
    near = 3 * nv - 1
    tiles_near = 2 * PT_DEV
    vmem = pltpu.VMEM
    dma = pltpu.SemaphoreType.DMA
    whole = pl.BlockSpec(memory_space=pltpu.VMEM)
    away = pl.BlockSpec(memory_space=pltpu.HBM)
    scratch = [
        vmem(masks.shape, jnp.int32),
        vmem(w_self.shape, BF16),
        vmem(w_col.shape, BF16),
        vmem(w_row.shape, BF16),
        vmem((slots, rows, cols, width), F32),
        vmem((slots, rows, cols, min(width, 128)), BF16),
        vmem((slots, nk, rows // group, chunk + 2 * group, group * chunk), BF16),
        vmem((nv * slots * part, tiles_near * part), BF16),
        vmem((tiles_near * part, 2 * nv * slots * part), BF16),
        vmem((nk, nv, slots, part, width), F32),
        vmem((nk, nv - 1, slots, part, width), F32),
        vmem((nk, tiles_near, part, width), F32),
        vmem((2, nk, tiles_near, part, width), F32),
        vmem((nk, nv - 1, slots, part, width), F32),
        vmem((nk, nv, slots, part, width), F32),
        vmem((slots, rows, width), F32),
        vmem((np_, share, width), F32),
        vmem((np_ - 1, share, width), F32),
        vmem((share, width), F32),
        vmem((np_ - 1, share, width), F32),
        vmem((VT_DEV, rows, width), F32),
        vmem((2 * slots, cols), F32),
        vmem((near, 2 * slots, cols), F32),
        vmem((np_, share, cols), F32),
        vmem((np_ - 1, share, cols), F32),
        vmem((tiles_near, cols, cols), F32),
        vmem((share, width), F32),
        dma((nk,)),
        dma((4,)),
        dma((nk, 2)), dma((2, nk, 2)), dma((nk, 2)),
        dma((2,)), dma((2,)), dma((2,)), dma((2,)),
    ]
    current = pl.pallas_call(
        functools.partial(layers_kernel, nv, np_, nk),
        out_shape=jax.ShapeDtypeStruct(features.shape, BF16),
        in_specs=[
            pl.BlockSpec(memory_space=pltpu.SMEM),
            away, away, away, away, away, whole,
        ],
        out_specs=whole,
        scratch_shapes=scratch,
        compiler_params=pltpu.CompilerParams(
            collective_id=0, has_side_effects=True, vmem_limit_bytes=44 * 1024 * 1024),
        name="layers",
    )(*[pltpu.with_memory_space_constraint(x, pltpu.HBM)
        for x in (tiles.T, features, masks, w_self, w_col, w_row, bias)])
    return pl.pallas_call(
        hand_over_kernel,
        out_shape=jax.ShapeDtypeStruct(features.shape, BF16),
        in_specs=[pl.BlockSpec(memory_space=pl.ANY)],
        out_specs=away,
        scratch_shapes=[dma((slots,))],
        compiler_params=pltpu.CompilerParams(vmem_limit_bytes=1024 * 1024),
        name="hand_over",
    )(current)


def solution(mesh):
    in_specs = (
        P(("view", "point"), None, None, None),
        P(("view", "point"), None),
        P(("view", "point"), None, None),
        P(), P(), P(), P(),
    )
    out_specs = P(("view", "point"), None, None, None)
    body = functools.partial(shards, mesh.shape["view"], mesh.shape["point"])
    return jax.shard_map(body, mesh=mesh, in_specs=in_specs, out_specs=out_specs, check_vma=False)
```

```python
import functools

import jax
import jax.numpy as jnp
from jax import lax
from jax.experimental import pallas as pl
from jax.experimental.pallas import tpu as pltpu
from jax.sharding import PartitionSpec as P

VT_DEV = 4
PT_DEV = 4
MESH = pl.DeviceIdType.MESH
F32 = jnp.float32
BF16 = jnp.bfloat16
BIG = 2.0 ** 100


def wide(x, width):
    reps = width // x.shape[-1]
    return x if reps == 1 else jnp.concatenate([x] * reps, axis=-1)


def paired(me, o, size):
    if size & (size - 1):
        return lax.rem(me + o, size)
    total = me * 0
    bit = 1
    while bit < size:
        mine = lax.rem(me // bit, 2)
        total = total + bit * (1 - mine if o & bit else mine)
        bit *= 2
    return total


def step_of(me, other, size):
    if size & (size - 1):
        return lax.rem(me - other + size, size)
    return paired(me, other, size)


def stage_order(nk):
    stages = []
    for k in range(nk):
        stages.append(("self", k))
        if k == 0:
            stages.append(("tables", 0))
        stages.append(("sum", k))
    stages.append(("row", 0))
    stages += [("project", k) for k in range(nk)]
    return stages + [("bound", i) for i in range(4)]


def layers_kernel(
    nv, np_, nk,
    tiles_ref, feat_ref, mask_hbm, wself_hbm, wcol_hbm, wrow_hbm, bias_ref,
    cur, self_tail, col_tail, row_tail,
    mask_ref, wself_ref, wcol_ref, wrow_ref, self_p, bound, pick, gather_mat, scatter_mat,
    col_send, rs_buf, total_buf, side_buf, ag_send, ag_buf,
    row_acc, row_send, row_rs, row_ag_send, row_ag, row_p,
    cm_send, cm_buf, ri_send, ri_buf, col_scale, row_scale,
    feat_sem, in_sem, rs_sem, side_sem, ag_sem, rr_sem, ra_sem, cm_sem, ri_sem,
):
    a = lax.axis_index("view")
    b = lax.axis_index("point")
    slots, rows, cols, width = cur.shape
    layers = wself_ref.shape[0]
    chunk = cols // nk
    part = chunk // nv
    share = row_send.shape[1]
    tiles_near = 2 * PT_DEV

    def view_at(o):
        return paired(a, o, nv)

    def fellow_at(o):
        return paired(b, o, np_)

    def point_at(o):
        return lax.rem(b + o + np_, np_)

    def remote(src, dst, sems, va, pb):
        return pltpu.make_async_remote_copy(
            src_ref=src, dst_ref=dst, send_sem=sems.at[0], recv_sem=sems.at[1],
            device_id=(va, pb), device_id_type=MESH,
        )

    def wait_all(landed, sems):
        for end in range(2):
            pltpu.make_async_copy(landed, landed, sems.at[end]).wait()

    def rs_copy(k, o):
        return remote(col_send.at[k, view_at(o)], rs_buf.at[k, o - 1],
                      rs_sem.at[k], view_at(o), b)

    def ag_copy(k, o):
        return remote(ag_send.at[k, o - 1], ag_buf.at[k, o],
                      ag_sem.at[k], view_at(o), b)

    def f_copy(turn, k):
        return remote(total_buf.at[k, pl.ds(PT_DEV, PT_DEV)], side_buf.at[turn, k, pl.ds(0, PT_DEV)],
                      side_sem.at[turn, k], a, point_at(1))

    def b_copy(turn, k):
        return remote(total_buf.at[k, pl.ds(0, PT_DEV)], side_buf.at[turn, k, pl.ds(PT_DEV, PT_DEV)],
                      side_sem.at[turn, k], a, point_at(-1))

    def rr_copy(o):
        return remote(row_send.at[fellow_at(o)], row_rs.at[o - 1],
                      rr_sem, a, fellow_at(o))

    def ra_copy(o):
        return remote(row_ag_send, row_ag.at[o - 1], ra_sem, a, fellow_at(o))

    near = [(o, d) for d in (0, 1, -1) for o in range(nv) if (o, d) != (0, 0)]

    def cm_copy(n):
        o, d = near[n]
        return remote(cm_send, cm_buf.at[n], cm_sem, view_at(o), point_at(d))

    def ri_copy(o):
        return remote(ri_send.at[fellow_at(o)], ri_buf.at[o - 1],
                      ri_sem, a, fellow_at(o))

    def feat_copy(k):
        span = pl.ds(k * chunk, chunk)
        return pltpu.make_async_copy(
            feat_ref.at[:, :, span, :], cur.at[:, :, span, :], feat_sem.at[k])

    def in_copy(n):
        src = (mask_hbm, wself_hbm, wcol_hbm, wrow_hbm)[n]
        dst = (mask_ref, wself_ref, wcol_ref, wrow_ref)[n]
        return pltpu.make_async_copy(src, dst, in_sem.at[n])

    in_copy(0).start()
    for k in range(nk):
        feat_copy(k).start()
    for n in range(1, 4):
        in_copy(n).start()

    barrier = pltpu.get_barrier_semaphore()
    friends = [(0, o) for o in range(2, np_ - 1)] + near
    for o, d in friends:
        pl.semaphore_signal(barrier, inc=1, device_id=(view_at(o), point_at(d)) if (o, d) in near
                            else (a, point_at(d)), device_id_type=MESH)
    in_copy(0).wait()

    group = pick.shape[4] // chunk
    lanes = cols

    for s in range(slots):
        cm_send[s:s + 1, :] = jnp.sum(mask_ref[s].astype(F32), axis=0, keepdims=True)
        cm_send[slots + s:slots + s + 1, :] = jnp.full(
            (1, lanes), tiles_ref[1, s], jnp.int32).astype(F32)
    for v in range(VT_DEV):
        total = jnp.zeros((rows, lanes), F32)
        for s in range(slots):
            rcount = jnp.broadcast_to(
                jnp.sum(mask_ref[s].astype(F32), axis=1, keepdims=True), (rows, lanes))
            hit = jnp.full((rows, lanes), tiles_ref[0, s], jnp.int32) == v
            total = total + jnp.where(hit, rcount, 0.0)
        for i in range(max(rows // share, 1)):
            at = v * rows + i * share
            ri_send[at // share] = total[i * share:(i + 1) * share]

    def build_pick(s, carry):
        shape = (group, group * chunk)
        lane = lax.broadcasted_iota(jnp.int32, shape, 1)
        of_view = lane // chunk == lax.broadcasted_iota(jnp.int32, shape, 0)
        shape = (chunk, group * chunk)
        lane = lax.broadcasted_iota(jnp.int32, shape, 1)
        of_point = lane % chunk == lax.broadcasted_iota(jnp.int32, shape, 0)
        for g in range(rows // group):
            m = mask_ref[s, g * group:(g + 1) * group, :].astype(F32)
            for k in range(nk):
                tiled = jnp.concatenate([m[:, k * chunk:(k + 1) * chunk]] * group, axis=1)
                by_view = jnp.where(of_view, tiled, 0.0)
                flat = jnp.sum(by_view, axis=0, keepdims=True)
                by_point = jnp.where(of_point, jnp.broadcast_to(flat, shape), 0.0)
                both = jnp.concatenate([by_point, by_view, jnp.ones_like(by_view)], axis=0)
                pick[s, k, g] = both.astype(BF16)
        return carry

    lax.fori_loop(0, slots, build_pick, 0)

    def sum_rows(k, s, value_of):
        col = jnp.zeros((chunk, width), F32)
        for g in range(rows // group):
            both = jnp.dot(pick[s, k, g], value_of(g), preferred_element_type=F32)
            col = col + both[:chunk]
            new = both[chunk:chunk + group]
            at = pl.ds(g * group, group)
            if k == 0:
                row_acc[s, at, :] = new
            else:
                row_acc[s, at, :] = row_acc[s, at, :] + new
        for j in range(nv):
            col_send[k, j, s] = col[j * part:(j + 1) * part]

    def entries(k, s, g):
        span = pl.ds(k * chunk, chunk)
        return cur[s, g * group:(g + 1) * group, span, :].reshape(group * chunk, width)

    def over_slots(slot):
        lax.fori_loop(0, slots, slot, 0, unroll=4 if slots % 4 == 0 else 1)

    def first_sums(k):
        def slot(s, carry):
            sum_rows(k, s, lambda g: entries(k, s, g))
            return carry
        over_slots(slot)

    def build_bound(k, half):
        shape = (2 * group, bound.shape[3])
        row = lax.broadcasted_iota(jnp.int32, shape, 0)
        ends = jnp.where(row < group, 2.0 * BIG, jnp.where(row == group, -BIG, 0.0)).astype(BF16)

        def slot(s, carry):
            for g in range(rows // group):
                x = lax.dot_general(
                    pick[s, k, g, chunk:, :], ends, (((0,), (0,)), ((), ())),
                    preferred_element_type=F32)
                bound[s, g * group:(g + 1) * group, pl.ds(k * chunk, chunk), :] = (
                    x.reshape(group, chunk, shape[1]).astype(BF16))
            return carry
        lax.fori_loop(half * slots // 2, (half + 1) * slots // 2, slot, 0, unroll=True)

    def self_project(layer, k, masked):
        span = pl.ds(k * chunk, chunk)

        def slot(s, carry):
            for g in range(rows // group):
                z = jnp.dot(entries(k, s, g), wself_ref[layer], preferred_element_type=F32)
                z = z.reshape(group, chunk, width)
                if masked:
                    z = jnp.minimum(z, wide(
                        bound[s, g * group:(g + 1) * group, span, :].astype(F32), width))
                if masked and k == nk - 1:
                    self_tail[s, g * group:(g + 1) * group] = z
                else:
                    self_p[s, g * group:(g + 1) * group, span, :] = z
            return carry
        over_slots(slot)

    def mix(k, s, g):
        span = pl.ds(k * chunk, chunk)
        v = tiles_ref[0, s]
        colp = jnp.concatenate(
            [ag_buf[k, step_of(a, j, nv), s] for j in range(nv)], axis=0)
        found = []
        for r in range(g * group, (g + 1) * group):
            rowp = jnp.broadcast_to(row_p[v, r:r + 1, :], (chunk, width))
            y = jnp.maximum((self_p[s, r, span, :] + colp + rowp).astype(BF16), 0)
            cur[s, r, span, :] = y
            found.append(y)
        return jnp.concatenate(found, axis=0)

    def layer_chunk(k):
        def slot(s, carry):
            sum_rows(k, s, lambda g: mix(k, s, g))
            return carry
        over_slots(slot)

    def last_chunk(k):
        def slot(s, carry):
            if k == nk - 1:
                col_tail[s] = jnp.concatenate(
                    [ag_buf[k, step_of(a, j, nv), s] for j in range(nv)], axis=0)
                row_tail[s] = row_p[tiles_ref[0, s]]
            else:
                for g in range(rows // group):
                    mix(k, s, g)
            return carry
        over_slots(slot)

    def send_rows():
        for v in range(VT_DEV):
            total = jnp.zeros((rows, width), F32)
            for s in range(slots):
                hit = jnp.full((rows, width), tiles_ref[0, s], jnp.int32) == v
                total = total + jnp.where(hit, row_acc[s], 0.0)
            for i in range(max(rows // share, 1)):
                at = v * rows + i * share
                row_send[at // share] = total[i * share:(i + 1) * share]
        for o in reversed(range(1, np_)):
            rr_copy(o).start()

    def send_cols(k):
        for o in reversed(range(1, nv)):
            rs_copy(k, o).start()

    def halves(x):
        high = x.astype(BF16)
        return jnp.concatenate([high, (x - high.astype(F32)).astype(BF16)], axis=0)

    for k in range(nk):
        feat_copy(k).wait()
        first_sums(k)
        if k == 0:
            pl.semaphore_wait(barrier, len(friends))
            for n in range(len(near)):
                cm_copy(n).start()
            for o in range(1, np_):
                ri_copy(o).start()
        if k == nk - 1:
            send_rows()
        send_cols(k)
    for n in range(1, 4):
        in_copy(n).wait()

    def stage_tables():
        wait_all(cm_buf, cm_sem)
        messages = {(0, 0): cm_send[...]}
        for n, at in enumerate(near):
            messages[at] = cm_buf[n]

        def tile_of(o, s):
            return messages[o, 0][slots + s:slots + s + 1, :]

        def lane_tiled(x, size):
            return x[:, :size] if size <= lanes else jnp.concatenate([x] * (size // lanes), axis=1)

        shape = scatter_mat.shape
        lane = lax.broadcasted_iota(jnp.int32, (1, shape[1]), 1) % (nv * slots * part)
        q_lane = jnp.zeros((1, shape[1]), F32)
        for o in range(nv):
            for s in range(slots):
                q_lane = jnp.where(lane // part == o * slots + s, lane_tiled(tile_of(o, s), shape[1]), q_lane)
        row = lax.broadcasted_iota(jnp.int32, shape, 0)
        lane = lax.broadcasted_iota(jnp.int32, shape, 1)
        hit = (jnp.broadcast_to(q_lane, shape) == (row // part).astype(F32)) & (row % part == lane % part)
        scatter_mat[...] = jnp.where(hit, 1.0, 0.0).astype(BF16)

        shape = (part, tiles_near * part)
        lane = lax.broadcasted_iota(jnp.int32, shape, 1)
        same = lane % part == lax.broadcasted_iota(jnp.int32, shape, 0)
        tile = (lane // part).astype(F32)
        found = []
        for o in range(nv):
            for s in range(slots):
                q = jnp.broadcast_to(lane_tiled(tile_of((nv - o) % nv if nv & (nv - 1) else o, s), shape[1]), shape)
                found.append(jnp.where((q == tile) & same, 1.0, 0.0))
        gather_mat[...] = jnp.concatenate(found, axis=0).astype(BF16)

        shape = (tiles_near, lanes)
        tile = lax.broadcasted_iota(jnp.int32, shape, 0).astype(F32)
        count = jnp.zeros(shape, F32)
        for (o, d), block in messages.items():
            for s in range(slots):
                q = jnp.broadcast_to(block[slots + s:slots + s + 1, :], shape)
                hit = q - float(d * PT_DEV) == tile
                count = count + jnp.where(hit, jnp.broadcast_to(block[s:s + 1, :], shape), 0.0)
        scale = (1.0 / jnp.sqrt(jnp.maximum(count, 1.0))).T
        for t in range(tiles_near):
            col_scale[t] = jnp.broadcast_to(scale[:, t:t + 1], (cols, lanes))

    def stage_row_scale():
        wait_all(ri_buf, ri_sem)
        total = ri_send[b]
        for o in range(1, np_):
            total = total + ri_buf[o - 1]
        row_scale[...] = wide(1.0 / jnp.sqrt(jnp.maximum(total, 1.0)), width)

    def stage_sum(turn, k):
        wait_all(rs_buf.at[k], rs_sem.at[k])
        blocks = [col_send[k, a] if o == 0 else rs_buf[k, o - 1] for o in range(nv)]
        blocks = jnp.concatenate([x.reshape(slots * part, width) for x in blocks], axis=0)
        total = jnp.dot(scatter_mat[...], halves(blocks), preferred_element_type=F32)
        total_buf[k] = total.reshape(tiles_near, part, width)
        f_copy(turn, k).start()
        b_copy(turn, k).start()

    def stage_project(layer, turn, k):
        wait_all(side_buf.at[turn, k], side_sem.at[turn, k])
        at = pl.multiple_of(k * chunk + a * part, part)
        scale = wide(col_scale[:, pl.ds(at, part), :], width)
        term = (total_buf[k] + side_buf[turn, k]) * scale
        term = term.reshape(tiles_near * part, width).astype(BF16)
        term = jnp.dot(gather_mat[...], term, preferred_element_type=F32).astype(BF16)
        chosen = jnp.dot(term, wcol_ref[layer], preferred_element_type=F32)
        chosen = chosen.reshape(nv, slots, part, width)
        ag_buf[k, 0] = chosen[0]
        for o in reversed(range(1, nv)):
            ag_send[k, o - 1] = chosen[o]
            ag_copy(k, o).start()

    def stage_row_project(layer):
        wait_all(row_rs, rr_sem)
        total = row_send[b]
        for o in range(1, np_):
            total = total + row_rs[o - 1]
        term = (total * row_scale[...]).astype(BF16)
        row_ag_send[...] = (
            jnp.dot(term, wrow_ref[layer], preferred_element_type=F32)
            + bias_ref[pl.ds(layer, 1), :])
        for o in reversed(range(1, np_)):
            ra_copy(o).start()

    def stage_row_collect():
        wait_all(row_ag, ra_sem)

        for j in range(np_):
            o = step_of(b, j, np_)
            got = row_ag[jnp.maximum(o - 1, 0)]
            block = jnp.where(jnp.full(got.shape, o, jnp.int32) == 0, row_ag_send[...], got)
            at = j * share
            row_p[at // rows, at % rows:at % rows + share, :] = block

    def exchange(layer, carry):
        turn = lax.rem(layer, 2)
        for name, k in stage_order(nk):
            if name == "sum":
                stage_sum(turn, k)
            elif name == "project":
                stage_project(layer, turn, k)
            elif name == "self":
                @pl.when(layer < layers - 1)
                def _():
                    self_project(layer, k, False)

                @pl.when(layer == layers - 1)
                def _():
                    self_project(layer, k, True)
            elif name == "tables":
                pl.when(layer == 0)(stage_tables)
            elif name == "bound":
                for early in range(shifts):
                    @pl.when(layer == early)
                    def _():
                        for piece in range(2 * nk):
                            if piece % (4 * shifts) == 4 * early + k:
                                build_bound(piece // 2, piece % 2)
            else:
                pl.when(layer == 0)(stage_row_scale)
                stage_row_project(layer)
        stage_row_collect()
        for k in range(nk):
            wait_all(ag_buf.at[k, pl.ds(1, nv - 1)], ag_sem.at[k])

            @pl.when(layer < layers - 1)
            def _():
                layer_chunk(k)
                if k == nk - 1:
                    send_rows()
                send_cols(k)

            @pl.when(layer == layers - 1)
            def _():
                last_chunk(k)
        return carry

    shifts = min(layers - 1, 2)
    if shifts == 0:
        for k in range(nk):
            for half in range(2):
                build_bound(k, half)
    lax.fori_loop(0, layers, exchange, 0)


def finish_kernel(cur_ref, self_ref, col_ref, row_ref, out_ref, tail, sem):
    slots, rows, chunk, width = self_ref.shape
    head = cur_ref.shape[2] - chunk
    copies = []
    for s in range(slots if head else 0):
        span = pl.ds(0, head)
        copies.append(pltpu.make_async_copy(
            cur_ref.at[s, :, span, :], out_ref.at[s, :, span, :], sem.at[s]))
        copies[-1].start()
    for s in range(slots):
        col = col_ref[s]
        for r in range(rows):
            row = jnp.broadcast_to(row_ref[s, r:r + 1, :], (chunk, width))
            tail[s, r] = jnp.maximum((self_ref[s, r] + col + row).astype(BF16), 0)
        copies.append(pltpu.make_async_copy(
            tail.at[s], out_ref.at[s, :, pl.ds(head, chunk), :], sem.at[slots + s]))
        copies[-1].start()
    for copy in copies:
        copy.wait()


def shards(nv, np_, features, tiles, masks, w_self, w_col, w_row, bias):
    slots, rows, cols, width = features.shape
    layers = w_self.shape[0]
    nk = max(cols // (8 * nv), 1)
    chunk = cols // nk
    part = chunk // nv
    share = VT_DEV * rows // np_
    group = 256 // chunk
    near = 3 * nv - 1
    tiles_near = 2 * PT_DEV
    vmem = pltpu.VMEM
    dma = pltpu.SemaphoreType.DMA
    whole = pl.BlockSpec(memory_space=pltpu.VMEM)
    away = pl.BlockSpec(memory_space=pltpu.HBM)
    scratch = [
        vmem(masks.shape, jnp.int32),
        vmem(w_self.shape, BF16),
        vmem(w_col.shape, BF16),
        vmem(w_row.shape, BF16),
        vmem((slots, rows, cols, width), F32),
        vmem((slots, rows, cols, min(width, 128)), BF16),
        vmem((slots, nk, rows // group, chunk + 2 * group, group * chunk), BF16),
        vmem((nv * slots * part, tiles_near * part), BF16),
        vmem((tiles_near * part, 2 * nv * slots * part), BF16),
        vmem((nk, nv, slots, part, width), F32),
        vmem((nk, nv - 1, slots, part, width), F32),
        vmem((nk, tiles_near, part, width), F32),
        vmem((2, nk, tiles_near, part, width), F32),
        vmem((nk, nv - 1, slots, part, width), F32),
        vmem((nk, nv, slots, part, width), F32),
        vmem((slots, rows, width), F32),
        vmem((np_, share, width), F32),
        vmem((np_ - 1, share, width), F32),
        vmem((share, width), F32),
        vmem((np_ - 1, share, width), F32),
        vmem((VT_DEV, rows, width), F32),
        vmem((2 * slots, cols), F32),
        vmem((near, 2 * slots, cols), F32),
        vmem((np_, share, cols), F32),
        vmem((np_ - 1, share, cols), F32),
        vmem((tiles_near, cols, cols), F32),
        vmem((share, width), F32),
        dma((nk,)),
        dma((4,)),
        dma((nk, 2)), dma((2, nk, 2)), dma((nk, 2)),
        dma((2,)), dma((2,)), dma((2,)), dma((2,)),
    ]
    outs = pl.pallas_call(
        functools.partial(layers_kernel, nv, np_, nk),
        out_shape=(
            jax.ShapeDtypeStruct(features.shape, BF16),
            jax.ShapeDtypeStruct((slots, rows, chunk, width), F32),
            jax.ShapeDtypeStruct((slots, chunk, width), F32),
            jax.ShapeDtypeStruct((slots, rows, width), F32),
        ),
        in_specs=[
            pl.BlockSpec(memory_space=pltpu.SMEM),
            away, away, away, away, away, whole,
        ],
        out_specs=(whole, whole, whole, whole),
        scratch_shapes=scratch,
        compiler_params=pltpu.CompilerParams(
            collective_id=0, has_side_effects=True, vmem_limit_bytes=40 * 1024 * 1024),
        name="layers",
    )(*[pltpu.with_memory_space_constraint(x, pltpu.HBM)
        for x in (tiles.T, features, masks, w_self, w_col, w_row, bias)])
    return pl.pallas_call(
        finish_kernel,
        out_shape=jax.ShapeDtypeStruct(features.shape, BF16),
        in_specs=[pl.BlockSpec(memory_space=pl.ANY), whole, whole, whole],
        out_specs=away,
        scratch_shapes=[vmem((slots, rows, chunk, width), BF16), dma((2 * slots,))],
        compiler_params=pltpu.CompilerParams(vmem_limit_bytes=6 * 1024 * 1024),
        name="finish",
    )(*outs)


def solution(mesh):
    in_specs = (
        P(("view", "point"), None, None, None),
        P(("view", "point"), None),
        P(("view", "point"), None, None),
        P(), P(), P(), P(),
    )
    out_specs = P(("view", "point"), None, None, None)
    body = functools.partial(shards, mesh.shape["view"], mesh.shape["point"])
    return jax.shard_map(body, mesh=mesh, in_specs=in_specs, out_specs=out_specs, check_vma=False)
```
